32 devices in a mesh: seg: 8 (over z, x), bank: 4 (over y, core).
Axes of the slice: x: 2, y: 2, z: 4, core: 2. Of those that a mesh axis runs over, the one named last changes fastest.
Arguments:
- strain: float32 [393216], P('seg'), may hold values from -24000 to 24000, as said below
- inv_asd: float32 [32768], replicated, may hold values from 0.3 to 3
- templates: bfloat16 [2, 8, 32768], P(None, 'bank'), may hold values from -6 to 6
- tmpl_len: int32 [8], P('bank'), may hold values from 2048 to 16384, as said below
- weights: float32 [8], P('bank'), may hold values from 0.2 to 5
- chirp_mass: float32 [8], P('bank'), may hold values from 10 to 60
- valid: int32 [384], P('seg'), may hold values 0 or 1
Outputs:
- log_like: float32 [393216], P(('seg', 'bank'))
- chirp_mean: float32 [393216], P(('seg', 'bank'))
- delay_mean: float32 [393216], P(('seg', 'bank'))
The draws below stay inside these ranges and needn't reach their ends.
Inputs may be any that keep to these rules, and one draw needn't show every extreme that they name: `strain`: noise amplitude may change from one block of 1024 samples to the next. `tmpl_len`: template lengths lie between 2048 and 16384 samples, both ends taken.
All inputs are finite; a program needn't handle non-finite values. No bound on the sum of `valid` on one device may be relied on, other than what follows from the above.
Results may differ from the reference program's by a relative error of at most 0.00035.
Values sent between devices are 32-bit elements; how exact they have to be, the bound alone decides.
No kernel may reach another device: no remote copies, remote signals or barrier semaphores. Data moves between devices by JAX's collectives and lax.ppermute only.
A program may use at most 64 MiB of HBM per device.

```python
import math
import jax
import jax.numpy as jnp
from jax import lax

NFFT = 65536
OVER = 16384
GATE = 1024
RATE = 4096
NBIN = 32768
HOP = 49152
TEMPLATES = 8
SAMPLES = 393216


def draw_strain(key, part):
    noise_key, level_key = jax.random.split(key, 2)
    block_count = SAMPLES // GATE
    noise = jnp.clip(jax.random.normal(noise_key, (SAMPLES,), jnp.float32), -8.0, 8.0)
    envelope = jnp.exp(jax.random.uniform(level_key, (block_count,), jnp.float32, math.log(0.5), math.log(2.0)))
    return (noise.reshape(block_count, GATE) * envelope[:, None]).reshape(SAMPLES)


def draw_tmpl_len(key, part):
    first_key, top_key, low_key = jax.random.split(jax.random.fold_in(key, 17), 3)
    lengths = jax.random.randint(first_key, (TEMPLATES,), OVER // 8, OVER + 1, jnp.int32)
    top_index = jax.random.randint(top_key, (), 0, TEMPLATES, jnp.int32)
    low_index = (top_index + 1 + jax.random.randint(low_key, (), 0, TEMPLATES - 1, jnp.int32)) % TEMPLATES
    positions = jnp.arange(TEMPLATES, dtype=jnp.int32)
    lengths = jnp.where(positions == top_index, OVER, lengths)
    lengths = jnp.where(positions == low_index, OVER // 8, lengths)
    return lengths.astype(jnp.int32)


def plant(values, key, smallest, high):
    dims = values.shape
    place = [jax.random.randint(jax.random.fold_in(key, axis), (), 0, dims[axis]) for axis in range(len(dims))]
    values = values.at[tuple(place)].set(smallest)
    longest = dims.index(max(dims))
    place[longest] = (place[longest] + 1) % dims[longest]
    return values.at[tuple(place)].set(high)


def block_scale(stream_key, dims, cuts, smallest, top_value):
    gain = 1.0
    for position, parts in cuts:
        steps = jax.random.uniform(jax.random.fold_in(jax.random.fold_in(stream_key, 6), position), (parts,), jnp.float32, smallest / len(cuts), top_value / len(cuts))
        gain = gain * jnp.repeat(jnp.exp(steps), dims[position] // parts).reshape((-1,) + (1,) * (len(dims) - 1 - position))
    return gain


def gaussian(key, shape, scale, limit, pieces=(), kind=jnp.bfloat16):
    result = jax.random.normal(key, shape, jnp.float32) * scale
    if len(pieces) > 0:
        result = block_scale(key, shape, pieces, -0.22, 0.18) * result
    return jnp.clip(result, min=-limit, max=limit).astype(kind)


def setup_inputs(seed: int = 0) -> dict:
    key_of = jax.random.split(jax.random.key(seed), 8)
    return {
        "strain": draw_strain(jax.random.fold_in(key_of[7], 71), 0),
        "inv_asd": jnp.clip(jnp.exp(jax.random.uniform(key_of[1], (NBIN,), jnp.float32, math.log(0.3), math.log(3.0))), 0.3, 3.0),
        "templates": gaussian(key_of[2], (2, TEMPLATES, NBIN), 1.0, 6.0, ((1, 4),)),
        "tmpl_len": draw_tmpl_len(jax.random.fold_in(key_of[7], 71), 0),
        "weights": jnp.clip(jnp.exp(math.log(5.0) - 3.218876 * jax.random.uniform(key_of[4], (TEMPLATES,), jnp.float32) ** block_scale(key_of[4], (TEMPLATES,), ((0, 4),), -0.2, 0.2)), 0.2, 5.0),
        "chirp_mass": jnp.clip(jnp.exp(math.log(60.0) - 1.7917595 * jax.random.uniform(key_of[5], (TEMPLATES,), jnp.float32) ** block_scale(key_of[5], (TEMPLATES,), ((0, 4),), -0.2, 0.2)), 10.0, 60.0),
        "valid": plant((jax.random.randint(key_of[6], (SAMPLES // GATE,), 0, 8) < 7).astype(jnp.int32), jax.random.fold_in(key_of[6], 1), 0, 1),
    }


def log_bessel(rho_val):
    small_x = jnp.minimum(rho_val, 3.75)
    small_t = (small_x / 3.75) ** 2
    small_poly = 1.0 + small_t * (3.5156229 + small_t * (3.0899424 + small_t * (1.2067492 + small_t * (0.2659732 + small_t * (0.0360768 + small_t * 0.0045813)))))
    large_x = jnp.maximum(rho_val, 3.75)
    large_q = 3.75 / large_x
    large_poly = 0.39894228 + large_q * (0.01328592 + large_q * (0.00225319 + large_q * (-0.00157565 + large_q * (0.00916281 + large_q * (-0.02057706 + large_q * (0.02635537 + large_q * (-0.01647633 + large_q * 0.00392377)))))))
    large_val = large_x - 0.5 * jnp.log(large_x) + jnp.log(large_poly)
    return jnp.where(rho_val < 3.75, jnp.log(small_poly), large_val)

def reference(strain, inv_asd, templates, tmpl_len, weights, chirp_mass, valid):
    gate_mask = jnp.repeat(valid.astype(strain.dtype), GATE)
    gated_data = strain * gate_mask
    padded = jnp.concatenate([jnp.zeros((OVER,), strain.dtype), gated_data])
    tmpl_re = templates[0].astype(jnp.float32)
    tmpl_im = templates[1].astype(jnp.float32)
    sigma_sq = lax.optimization_barrier(jnp.sum((inv_asd * inv_asd)[None, :] * (tmpl_re * tmpl_re + tmpl_im * tmpl_im), axis=1))
    starts = (OVER - tmpl_len).astype(jnp.int32)
    delays = tmpl_len.astype(jnp.float32) / RATE
    prior_sum = jnp.sum(weights)

    def pick_row(score_row, begin_at):
        return lax.dynamic_slice_in_dim(score_row, begin_at, HOP)

    def per_segment(segment):
        window = lax.dynamic_slice_in_dim(padded, segment * HOP, NFFT)
        spectrum = jnp.fft.fft(window)[:NBIN] * inv_asd / math.sqrt(NFFT)
        spec_re = jnp.real(spectrum)
        spec_im = jnp.imag(spectrum)
        prod_re = spec_re[None, :] * tmpl_re + spec_im[None, :] * tmpl_im
        prod_im = spec_im[None, :] * tmpl_re - spec_re[None, :] * tmpl_im
        padded_bins = jnp.pad(prod_re + 1j * prod_im, ((0, 0), (0, NFFT - NBIN)))
        corr = jnp.fft.ifft(padded_bins, axis=1) * NFFT
        power = jnp.real(corr) ** 2 + jnp.imag(corr) ** 2
        rho_val = jnp.sqrt(power / sigma_sq[:, None])
        scores = log_bessel(rho_val)
        aligned = jax.vmap(pick_row)(scores, starts)
        peak_score = lax.optimization_barrier(jnp.max(aligned, axis=0))
        masses = weights[:, None] * jnp.exp(aligned - peak_score[None, :])
        total = lax.optimization_barrier(jnp.sum(masses, axis=0))
        chirp_sum = lax.optimization_barrier(jnp.sum(masses * chirp_mass[:, None], axis=0))
        delay_sum = lax.optimization_barrier(jnp.sum(masses * delays[:, None], axis=0))
        return (peak_score + jnp.log(total) - jnp.log(prior_sum), chirp_sum / total, delay_sum / total)
    segments = jnp.arange(SAMPLES // HOP, dtype=jnp.int32)
    log_like, chirp_mean, delay_mean = lax.map(per_segment, segments)
    return (log_like.reshape(-1), chirp_mean.reshape(-1), delay_mean.reshape(-1))
```

```python
import functools
import math

import jax
import jax.numpy as jnp
import numpy as np
from jax import lax
from jax.experimental import pallas as pl
from jax.experimental.pallas import tpu as pltpu
from jax.sharding import PartitionSpec as P

NFFT = 65536
FA = 256
HALF = 128
OVER = 16384
RATE = 4096
LANES = 128
F32 = jnp.float32
BF16 = jnp.bfloat16

TERMS = ((0, 0), (0, 1), (1, 0), (1, 1), (0, 2), (2, 0))
PARTS = 1 + max(max(term) for term in TERMS)


def parts_of_table(table):
    rest = np.asarray(table, np.float32)
    parts = []
    for _ in range(PARTS):
        part = rest.astype(jnp.bfloat16)
        parts.append(part)
        rest = rest - part.astype(np.float32)
    return parts


@functools.cache
def tables():
    index = np.arange(FA, dtype=np.int64)
    grid = index[:, None] * index[None, :]
    angle = (grid % FA) * (2.0 * math.pi / FA)
    cos_parts = parts_of_table(np.cos(angle))
    sin_parts = parts_of_table(np.sin(angle))
    neg_parts = [-part for part in sin_parts]
    fine = grid * (2.0 * math.pi / NFFT)
    twist = np.stack([np.cos(fine), np.sin(fine)]).astype(np.float32)
    rows = OVER // FA
    head = np.concatenate(
        [np.concatenate([cos_parts[i][:, :rows], neg_parts[i][:, :rows]]) for i, _ in TERMS], axis=1
    )
    return {
        "dft": np.stack([np.stack(cos_parts), np.stack(sin_parts), np.stack(neg_parts)]),
        "twist": twist,
        "head": head,
    }


def split(value):
    parts = []
    for step in range(PARTS):
        part = value.astype(BF16)
        parts.append(part)
        if step < PARTS - 1:
            value = value - part.astype(F32)
    return parts


def dot(left, right):
    return lax.dot_general(left, right, (((1,), (0,)), ((), ())), preferred_element_type=F32)


def dot_parts(left, right):
    return dot(
        jnp.concatenate([left[i] for i, _ in TERMS], axis=1),
        jnp.concatenate([right[j] for _, j in TERMS], axis=0),
    )


def log_bessel(power):
    inv = lax.rsqrt(jnp.maximum(power, 1e-30))
    rho = power * inv
    small = rho < 3.75
    t = jnp.minimum(power, 3.75 * 3.75) * (1.0 / (3.75 * 3.75))
    small_poly = 1.0 + t * (
        3.5156229
        + t * (3.0899424 + t * (1.2067492 + t * (0.2659732 + t * (0.0360768 + t * 0.0045813))))
    )
    q = jnp.minimum(3.75 * inv, 1.0)
    large_poly = 0.39894228 + q * (
        0.01328592
        + q
        * (
            0.00225319
            + q
            * (
                -0.00157565
                + q
                * (
                    0.00916281
                    + q
                    * (-0.02057706 + q * (0.02635537 + q * (-0.01647633 + q * 0.00392377)))
                )
            )
        )
    )
    inner = jnp.where(small, small_poly, large_poly * lax.rsqrt(jnp.maximum(rho, 3.75)))
    return jnp.where(small, 0.0, rho) + jnp.log(inner)


def turn_vector(period, shift):
    lane = lax.broadcasted_iota(jnp.int32, (1, LANES), 1)
    return lane, period, shift


def phase(index, period):
    wrapped = ((index + period // 2) & (period - 1)) - period // 2
    angle = wrapped.astype(F32) * (2.0 * math.pi / period)
    return jnp.cos(angle), jnp.sin(angle)


def tail_kernel(valid_ref, strain_ref, out_ref):
    rows = out_ref.shape[0]
    first = valid_ref.shape[0] - rows // 8
    for i in range(rows // 8):
        out_ref[8 * i : 8 * i + 8, :] = strain_ref[8 * i : 8 * i + 8, :] * valid_ref[
            first + i
        ].astype(F32)


def early_kernel(len_ref, valid_ref, strain_ref, asd_ref, tmpl_ref, dft_ref, section_ref, bank_ref, gated):
    rows = strain_ref.shape[0]
    for i in range(rows // 8):
        gated[8 * i : 8 * i + 8, :] = strain_ref[8 * i : 8 * i + 8, :] * valid_ref[i].astype(F32)
    frame = jnp.concatenate(
        [gated[pl.ds(0, rows // 2, stride=2), :], gated[pl.ds(1, rows // 2, stride=2), :]], axis=1
    )
    pad = jnp.zeros((FA - rows // 2, FA), BF16)
    frame_parts = [jnp.concatenate([pad, part], axis=0) for part in split(frame)]
    section_ref[0] = dot_parts([dft_ref[0, p] for p in range(PARTS)], frame_parts)
    section_ref[1] = dot_parts([dft_ref[2, p] for p in range(PARTS)], frame_parts)
    lane = lax.broadcasted_iota(jnp.int32, (1, LANES), 1)
    asd = [asd_ref[pl.ds(h, HALF, stride=2), :] for h in range(2)]
    for k in range(tmpl_ref.shape[1]):
        start = OVER - len_ref[k]
        col_cos, col_sin = phase(lane * start, FA)
        energy = jnp.zeros((1, 1), F32)
        turned = []
        for h in range(2):
            re = tmpl_ref[0, k, pl.ds(h, HALF, stride=2), :] * asd[h]
            im = tmpl_ref[1, k, pl.ds(h, HALF, stride=2), :] * asd[h]
            energy += jnp.sum(re * re + im * im, keepdims=True)
            row_cos, row_sin = phase((lane + h * LANES) * start, NFFT)
            new_re = (re * row_cos + im * row_sin).T
            new_im = (re * row_sin - im * row_cos).T
            turned.append((new_re, new_im))
        scale = lax.rsqrt(energy) * (1.0 / math.sqrt(NFFT))
        for h in range(2):
            new_re, new_im = turned[h]
            here = slice(h * HALF, h * HALF + HALF)
            bank_ref[k, here, :HALF] = (new_re * col_cos - new_im * col_sin) * scale
            bank_ref[k, here, HALF:] = (new_re * col_sin + new_im * col_cos) * scale


def spectrum_of(tail_ref, section_ref, head_ref, dft_ref, twist_ref):
    rows = tail_ref.shape[0]
    tail = jnp.concatenate(
        [tail_ref[pl.ds(0, rows // 2, stride=2), :], tail_ref[pl.ds(1, rows // 2, stride=2), :]],
        axis=1,
    )
    tail_parts = split(tail)
    extra = dot(head_ref[...], jnp.concatenate([tail_parts[j] for _, j in TERMS], axis=0))
    re = section_ref[0] + extra[:FA]
    im = section_ref[1] + extra[FA:]
    turn_cos, turn_sin = twist_ref[0], twist_ref[1]
    turned = jnp.concatenate([re * turn_cos + im * turn_sin, im * turn_cos - re * turn_sin], axis=1)
    right = [
        jnp.concatenate(
            [
                jnp.concatenate([dft_ref[0, p, :, :HALF], dft_ref[2, p, :, :HALF]], axis=1),
                jnp.concatenate([dft_ref[1, p, :, :HALF], dft_ref[0, p, :, :HALF]], axis=1),
            ],
            axis=0,
        )
        for p in range(PARTS)
    ]
    return dot_parts(split(turned), right)


def scores_of(spec, bank_k, dft_ref, twist_ref, rows):
    spec_re, spec_im = spec[:, :HALF], spec[:, HALF:]
    bank_re, bank_im = bank_k[:, :HALF], bank_k[:, HALF:]
    prod = jnp.concatenate(
        [spec_re * bank_re - spec_im * bank_im, spec_re * bank_im + spec_im * bank_re], axis=1
    )
    right = [
        jnp.concatenate(
            [
                jnp.concatenate([dft_ref[0, p, :HALF, :], dft_ref[1, p, :HALF, :]], axis=1),
                jnp.concatenate([dft_ref[2, p, :HALF, :], dft_ref[0, p, :HALF, :]], axis=1),
            ],
            axis=0,
        )
        for p in range(PARTS)
    ]
    inner = dot_parts(split(prod), right)
    in_re, in_im = inner[:, :FA], inner[:, FA:]
    turn_cos, turn_sin = twist_ref[0], twist_ref[1]
    twisted = split(
        jnp.concatenate([in_re * turn_cos - in_im * turn_sin, in_re * turn_sin + in_im * turn_cos], axis=0)
    )
    corr_re = dot_parts(
        [jnp.concatenate([dft_ref[0, p, :rows, :], dft_ref[2, p, :rows, :]], axis=1) for p in range(PARTS)],
        twisted,
    )
    corr_im = dot_parts(
        [jnp.concatenate([dft_ref[1, p, :rows, :], dft_ref[0, p, :rows, :]], axis=1) for p in range(PARTS)],
        twisted,
    )
    return log_bessel(corr_re * corr_re + corr_im * corr_im)


def traits_tile(len_ref, weight_ref, chirp_ref, count):
    rows = trait_rows(count)
    row = lax.broadcasted_iota(jnp.int32, (rows, LANES), 0)
    tile = jnp.zeros((rows, LANES), F32)
    for k in range(count):
        tile = jnp.where(row == 3 * k, weight_ref[k], tile)
        tile = jnp.where(row == 3 * k + 1, chirp_ref[k], tile)
        tile = jnp.where(row == 3 * k + 2, len_ref[k].astype(F32) / RATE, tile)
    return tile


def trait_rows(count):
    return (3 * count + 7) // 8 * 8


def partner(me, r, n):
    return me ^ r if n & (n - 1) == 0 else (me + r) % n


def main_kernel(
    len_ref, weight_ref, chirp_ref, tail_ref, section_ref, bank_ref, head_ref, dft_ref, twist_ref, *refs
):
    n = len(refs) - 1
    outs, scores = refs[:n], refs[n]
    count, rows = bank_ref.shape[0], scores.shape[1]
    me = lax.axis_index("bank")
    spec = spectrum_of(tail_ref, section_ref, head_ref, dft_ref, twist_ref)
    for k in range(count):
        score = scores_of(spec, bank_ref[k], dft_ref, twist_ref, rows // 2)
        scores[k, pl.ds(0, rows // 2, stride=2), :] = score[:, :LANES]
        scores[k, pl.ds(1, rows // 2, stride=2), :] = score[:, LANES:]
    share = rows // n
    tile = traits_tile(len_ref, weight_ref, chirp_ref, count)
    for r in range(n):
        begin = pl.multiple_of(partner(me, r, n) * share, 8)
        for k in range(count):
            outs[r][k * share : (k + 1) * share, :] = scores[k, pl.ds(begin, share), :]
        outs[r][count * share :, :] = tile


def final_kernel(*refs):
    *banks, log_ref, chirp_ref, delay_ref = refs
    share = log_ref.shape[0]
    count = banks[0].shape[0] // share
    entries = [
        (
            bank[k * share : (k + 1) * share, :],
            *(bank[count * share + 3 * k + i : count * share + 3 * k + i + 1, :] for i in range(3)),
        )
        for bank in banks
        for k in range(count)
    ]
    peak = functools.reduce(jnp.maximum, [entry[0] for entry in entries])
    masses = [entry[1] * jnp.exp(entry[0] - peak) for entry in entries]
    total = functools.reduce(jnp.add, masses)
    chirp = functools.reduce(jnp.add, [mass * entry[2] for mass, entry in zip(masses, entries)])
    delay = functools.reduce(jnp.add, [mass * entry[3] for mass, entry in zip(masses, entries)])
    prior = functools.reduce(jnp.add, [entry[1] for entry in entries])
    log_ref[...] = peak + jnp.log(total) - jnp.log(prior)
    inv = 1.0 / total
    chirp_ref[...] = chirp * inv
    delay_ref[...] = delay * inv


SMEM = pl.BlockSpec(memory_space=pltpu.SMEM)
VMEM = pl.BlockSpec(memory_space=pltpu.VMEM)
VMEM_LIMIT = 60 * 1024 * 1024


def params():
    return pltpu.CompilerParams(vmem_limit_bytes=VMEM_LIMIT)


def local(strain, inv_asd, templates, tmpl_len, weights, chirp_mass, valid):
    n = lax.axis_size("bank")
    segs = lax.axis_size("seg")
    count = templates.shape[1]
    rows = strain.shape[0] // LANES
    tail_rows = OVER // LANES
    table = tables()
    dft, twist, head = (jnp.asarray(table[key]) for key in ("dft", "twist", "head"))
    strain = strain.reshape(rows, LANES)
    tail = pl.pallas_call(
        tail_kernel,
        grid=(1,),
        in_specs=[SMEM, pl.BlockSpec((tail_rows, LANES), lambda i: (rows // tail_rows - 1, 0))],
        out_specs=VMEM,
        out_shape=pltpu.VMEM((tail_rows, LANES), F32),
        name="tail",
    )(valid, strain)
    halo = lax.ppermute(tail, "seg", [(i, i + 1) for i in range(segs - 1)])
    section, bank = pl.pallas_call(
        early_kernel,
        in_specs=[SMEM, SMEM, VMEM, VMEM, VMEM, VMEM],
        out_specs=[VMEM, VMEM],
        out_shape=[pltpu.VMEM((2, FA, FA), F32), pltpu.VMEM((count, FA, FA), F32)],
        scratch_shapes=[pltpu.VMEM((rows, LANES), F32)],
        compiler_params=params(),
        cost_estimate=pl.CostEstimate(flops=2 * 10**9, bytes_accessed=2 * 10**6, transcendentals=0),
        name="early",
    )(
        tmpl_len,
        valid,
        strain,
        inv_asd.reshape(-1, LANES),
        templates.astype(F32).reshape(2, count, -1, LANES),
        dft,
    )
    share = rows // n
    chunk = (count * share + trait_rows(count), LANES)
    outs = pl.pallas_call(
        main_kernel,
        in_specs=[SMEM] * 3 + [VMEM] * 6,
        out_specs=[VMEM] * n,
        out_shape=[pltpu.VMEM(chunk, F32)] * n,
        scratch_shapes=[pltpu.VMEM((count, rows, LANES), F32)],
        compiler_params=params(),
        cost_estimate=pl.CostEstimate(flops=4 * 10**9, bytes_accessed=4 * 10**6, transcendentals=0),
        name="main",
    )(tmpl_len, weights, chirp_mass, halo, section, bank, head, dft, twist)
    banks = [outs[0]] + [
        lax.ppermute(outs[r], "bank", [(i, partner(i, r, n)) for i in range(n)]) for r in range(1, n)
    ]
    results = pl.pallas_call(
        final_kernel,
        in_specs=[VMEM] * n,
        out_specs=[VMEM] * 3,
        out_shape=[jax.ShapeDtypeStruct((share, LANES), F32)] * 3,
        compiler_params=params(),
        name="final",
    )(*banks)
    return tuple(result.reshape(-1) for result in results)


def solution(mesh):
    placed = (P("seg"), P(), P(None, "bank", None), P("bank"), P("bank"), P("bank"), P("seg"))
    return jax.shard_map(
        local,
        mesh=mesh,
        in_specs=placed,
        out_specs=(P(("seg", "bank")), P(("seg", "bank")), P(("seg", "bank"))),
        check_vma=False,
    )
```

```python
import functools
import math

import jax
import jax.numpy as jnp
import numpy as np
from jax import lax
from jax.experimental import pallas as pl
from jax.experimental.pallas import tpu as pltpu
from jax.sharding import PartitionSpec as P

NFFT = 65536
FA = 256
HALF = 128
OVER = 16384
RATE = 4096
LANES = 128
F32 = jnp.float32
BF16 = jnp.bfloat16

TERMS = ((0, 0), (0, 1), (1, 0), (1, 1), (0, 2), (2, 0))
PARTS = 1 + max(max(term) for term in TERMS)


def parts_of_table(table):
    rest = np.asarray(table, np.float32)
    parts = []
    for _ in range(PARTS):
        part = rest.astype(jnp.bfloat16)
        parts.append(part)
        rest = rest - part.astype(np.float32)
    return parts


def complex_rows(angle, sign):
    cos, sin = np.cos(angle), sign * np.sin(angle)
    return np.block([[cos, -sin], [sin, cos]])


@functools.cache
def tables(hop_rows):
    index = np.arange(FA)
    grid = index[:, None] * index[None, :]
    full = 2.0 * math.pi / FA
    first = parts_of_table(np.concatenate([np.cos(grid % FA * full), -np.sin(grid % FA * full)]))
    rows = OVER // FA
    head = np.concatenate([first[i][:, :rows] for i, _ in TERMS], axis=1)
    quarter = np.arange(FA // 4)
    second = np.concatenate(
        [
            complex_rows((2 * quarter[:, None] + odd) * index[None, :] % FA * full, -1.0).T
            for odd in range(2)
        ],
        axis=1,
    )
    second = np.concatenate([part for part in parts_of_table(second)])
    third = []
    for odd in range(2):
        angle = index[:HALF, None] * (2 * quarter[None, :] + odd) % FA * full
        parts = parts_of_table(complex_rows(angle, 1.0).T)
        third.append(np.stack(parts))
    angle = np.arange(hop_rows // 2)[:, None] * index[None, :HALF] % HALF * (2.0 * full)
    fourth = parts_of_table(complex_rows(angle, 1.0))
    fine = grid * (2.0 * math.pi / NFFT)
    turn = np.repeat(index[:HALF, None] * full, LANES, axis=1)
    return {
        "first": np.stack(first),
        "head": head,
        "second": second.reshape(PARTS, 2 * FA, FA),
        "third": np.stack(third),
        "fourth": np.stack(fourth),
        "twist": np.stack([np.cos(fine), np.sin(fine)]).astype(np.float32),
        "turn": np.stack([np.cos(turn), np.sin(turn)]).astype(np.float32),
    }


def split(value):
    parts = []
    for step in range(PARTS):
        part = value.astype(BF16)
        parts.append(part)
        if step < PARTS - 1:
            value = value - part.astype(F32)
    return parts


def dot(left, right):
    return lax.dot_general(left, right, (((1,), (0,)), ((), ())), preferred_element_type=F32)


def left_terms(parts):
    return jnp.concatenate([parts[i] for i, _ in TERMS], axis=1)


def right_terms(parts):
    return jnp.concatenate([parts[j] for _, j in TERMS], axis=0)


def log_bessel(power):
    inv = lax.rsqrt(jnp.maximum(power, 1e-30))
    rho = power * inv
    small = rho < 3.75
    t = jnp.minimum(power, 3.75 * 3.75) * (1.0 / (3.75 * 3.75))
    small_poly = 1.0 + t * (
        3.5156229
        + t * (3.0899424 + t * (1.2067492 + t * (0.2659732 + t * (0.0360768 + t * 0.0045813))))
    )
    q = jnp.minimum(3.75 * inv, 1.0)
    large_poly = 0.39894228 + q * (
        0.01328592
        + q
        * (
            0.00225319
            + q
            * (
                -0.00157565
                + q
                * (
                    0.00916281
                    + q
                    * (-0.02057706 + q * (0.02635537 + q * (-0.01647633 + q * 0.00392377)))
                )
            )
        )
    )
    inner = jnp.where(small, small_poly, large_poly * lax.rsqrt(jnp.maximum(rho, 3.75)))
    return jnp.where(small, 0.0, rho) + jnp.log(inner)


def phase(index, period):
    wrapped = ((index + period // 2) & (period - 1)) - period // 2
    angle = wrapped.astype(F32) * (2.0 * math.pi / period)
    return jnp.cos(angle), jnp.sin(angle)


def gate(target, source, flags, first):
    for i in range(target.shape[0] // 8):
        here = slice(8 * i, 8 * i + 8)
        target[here, :] = source[here, :] * flags[first + i].astype(F32)


def frame_of(samples):
    rows = samples.shape[0] // 2
    return jnp.concatenate([samples[pl.ds(h, rows, stride=2), :] for h in range(2)], axis=1)


def tail_kernel(valid_hbm, strain_hbm, out_ref, samples, flags, sems):
    rows = samples.shape[0]
    copies = [
        pltpu.make_async_copy(strain_hbm.at[pl.ds(strain_hbm.shape[0] - rows, rows), :], samples, sems.at[0]),
        pltpu.make_async_copy(valid_hbm, flags, sems.at[1]),
    ]
    for copy in copies:
        copy.start()
    for copy in copies:
        copy.wait()
    gate(out_ref, samples, flags, flags.shape[0] - rows // 8)


def early_kernel(
    len_hbm,
    weight_hbm,
    chirp_hbm,
    valid_hbm,
    strain_hbm,
    asd_hbm,
    first_hbm,
    tmpl_ref,
    section_ref,
    bank_ref,
    traits_ref,
    lens,
    weights,
    chirps,
    flags,
    samples,
    gated,
    asd_v,
    first_v,
    sems,
):
    pairs = (
        (strain_hbm, samples),
        (valid_hbm, flags),
        (first_hbm, first_v),
        (asd_hbm, asd_v),
        (len_hbm, lens),
        (weight_hbm, weights),
        (chirp_hbm, chirps),
    )
    copies = [pltpu.make_async_copy(a, b, sems.at[i]) for i, (a, b) in enumerate(pairs)]
    for copy in copies:
        copy.start()
    for copy in copies:
        copy.wait()
    gate(gated, samples, flags, 0)
    frame = frame_of(gated)
    pad = jnp.zeros((FA - frame.shape[0], FA), BF16)
    frame_parts = [jnp.concatenate([pad, part], axis=0) for part in split(frame)]
    section_ref[...] = dot(left_terms([first_v[p] for p in range(PARTS)]), right_terms(frame_parts))
    traits_ref[...] = traits_tile(lens, weights, chirps, tmpl_ref.shape[1])
    lane = lax.broadcasted_iota(jnp.int32, (1, LANES), 1)
    quarter = FA // 4
    sign = jnp.where(lane < quarter, 1.0, -1.0)
    blocks = [(q, h) for q in range(2) for h in range(2)]
    asd = {(q, h): asd_v[pl.ds(2 * q + h, quarter, stride=4), :] for q, h in blocks}
    for k in range(tmpl_ref.shape[1]):
        start = OVER - lens[k]
        energy = jnp.zeros((1, 1), F32)
        turned = {}
        for q, h in blocks:
            re = tmpl_ref[0, k, pl.ds(2 * q + h, quarter, stride=4), :] * asd[q, h]
            im = tmpl_ref[1, k, pl.ds(2 * q + h, quarter, stride=4), :] * asd[q, h]
            energy += jnp.sum(re * re + im * im, keepdims=True)
            row_cos, row_sin = phase((lane + h * LANES) * start, NFFT)
            new_re = re * row_cos + im * row_sin
            new_im = re * row_sin - im * row_cos
            turned[q, h] = (
                jnp.concatenate([new_re, new_re], axis=0).T,
                jnp.concatenate([-new_im, new_im], axis=0).T,
            )
        scale = lax.rsqrt(energy) * (1.0 / math.sqrt(NFFT))
        for q in range(2):
            col_cos, col_sin = phase((2 * (lane & (quarter - 1)) + q) * start, FA)
            col_cos, col_sin = col_cos * scale, col_sin * sign * scale
            for h in range(2):
                own, cross = turned[q, h]
                rows, cols = slice(h * HALF, h * HALF + HALF), slice(q * LANES, q * LANES + LANES)
                bank_ref[k, 0, rows, cols] = own * col_cos + cross * col_sin
                bank_ref[k, 1, rows, cols] = cross * col_cos - own * col_sin


def spectrum_of(tail_ref, section_ref, head_ref, second_ref, twist_ref):
    section = section_ref[...] + dot(head_ref[...], right_terms(split(frame_of(tail_ref))))
    re, im = section[:FA], section[FA:]
    turn_cos, turn_sin = twist_ref[0], twist_ref[1]
    turned = jnp.concatenate([re * turn_cos + im * turn_sin, im * turn_cos - re * turn_sin], axis=1)
    return dot(left_terms(split(turned)), right_terms([second_ref[p] for p in range(PARTS)]))


def swapped(value):
    return jnp.concatenate(
        [pltpu.roll(value[:, i : i + LANES], LANES // 2, axis=1) for i in range(0, value.shape[1], LANES)],
        axis=1,
    )


def scores_of(spec, spec_swapped, bank_ref, k, third_ref, fourth_ref, twist_ref, turn_ref):
    prod = spec * bank_ref[k, 0] + spec_swapped * bank_ref[k, 1]
    even = dot(left_terms(split(prod[:, :LANES])), right_terms([third_ref[0, p] for p in range(PARTS)]))
    odd = dot(left_terms(split(prod[:, LANES:])), right_terms([third_ref[1, p] for p in range(PARTS)]))
    plus, minus = even + odd, even - odd
    in_re = jnp.concatenate([plus[:, :HALF], minus[:, :HALF]], axis=1)
    in_im = jnp.concatenate([plus[:, HALF:], minus[:, HALF:]], axis=1)
    turn_cos, turn_sin = twist_ref[0], twist_ref[1]
    out_re = in_re * turn_cos - in_im * turn_sin
    out_im = in_re * turn_sin + in_im * turn_cos
    sum_re, sum_im = out_re[:HALF] + out_re[HALF:], out_im[:HALF] + out_im[HALF:]
    gap_re, gap_im = out_re[:HALF] - out_re[HALF:], out_im[:HALF] - out_im[HALF:]
    half_cos = jnp.concatenate([turn_ref[0]] * 2, axis=1)
    half_sin = jnp.concatenate([turn_ref[1]] * 2, axis=1)
    odd_re, odd_im = gap_re * half_cos - gap_im * half_sin, gap_re * half_sin + gap_im * half_cos
    pieces = [jnp.concatenate([sum_re, sum_im], axis=0), jnp.concatenate([odd_re, odd_im], axis=0)]
    scores = []
    for piece in pieces:
        corr = dot(left_terms([fourth_ref[p] for p in range(PARTS)]), right_terms(split(piece)))
        rows = corr.shape[0] // 2
        re, im = corr[:rows], corr[rows:]
        scores.append(log_bessel(re * re + im * im))
    return scores


def traits_tile(lens, weights, chirps, count):
    rows = trait_rows(count)
    row = lax.broadcasted_iota(jnp.int32, (rows, LANES), 0)
    tile = jnp.zeros((rows, LANES), F32)
    for k in range(count):
        tile = jnp.where(row == 3 * k, weights[k], tile)
        tile = jnp.where(row == 3 * k + 1, chirps[k], tile)
        tile = jnp.where(row == 3 * k + 2, lens[k].astype(F32) / RATE, tile)
    return tile


def trait_rows(count):
    return (3 * count + 7) // 8 * 8


def partner(me, r, n):
    return me ^ r if n & (n - 1) == 0 else (me + r) % n


def main_kernel(
    tail_ref,
    section_ref,
    bank_ref,
    traits_ref,
    head_ref,
    second_ref,
    third_ref,
    fourth_ref,
    twist_ref,
    turn_ref,
    *refs,
):
    n = len(refs) - 1
    outs, scores = refs[:n], refs[n]
    count, rows = bank_ref.shape[0], scores.shape[1]
    me = lax.axis_index("bank")
    spec = spectrum_of(tail_ref, section_ref, head_ref, second_ref, twist_ref)
    spec_swapped = swapped(spec)
    for k in range(count):
        pair = scores_of(spec, spec_swapped, bank_ref, k, third_ref, fourth_ref, twist_ref, turn_ref)
        for q, score in enumerate(pair):
            for h in range(2):
                scores[k, pl.ds(2 * q + h, rows // 4, stride=4), :] = score[:, h * LANES : (h + 1) * LANES]
    share = rows // n
    for r in range(n):
        begin = pl.multiple_of(partner(me, r, n) * share, 8)
        for k in range(count):
            outs[r][k * share : (k + 1) * share, :] = scores[k, pl.ds(begin, share), :]
        outs[r][count * share :, :] = traits_ref[...]


def final_kernel(*refs):
    *banks, log_ref, chirp_ref, delay_ref = refs
    share = log_ref.shape[0]
    count = banks[0].shape[0] // share
    entries = [
        (
            bank[k * share : (k + 1) * share, :],
            *(bank[count * share + 3 * k + i : count * share + 3 * k + i + 1, :] for i in range(3)),
        )
        for bank in banks
        for k in range(count)
    ]
    peak = functools.reduce(jnp.maximum, [entry[0] for entry in entries])
    masses = [entry[1] * jnp.exp(entry[0] - peak) for entry in entries]
    total = functools.reduce(jnp.add, masses)
    chirp = functools.reduce(jnp.add, [mass * entry[2] for mass, entry in zip(masses, entries)])
    delay = functools.reduce(jnp.add, [mass * entry[3] for mass, entry in zip(masses, entries)])
    prior = functools.reduce(jnp.add, [entry[1] for entry in entries])
    log_ref[...] = peak + jnp.log(total) - jnp.log(prior)
    inv = 1.0 / total
    chirp_ref[...] = chirp * inv
    delay_ref[...] = delay * inv


HBM = pl.BlockSpec(memory_space=pltpu.HBM)
VMEM = pl.BlockSpec(memory_space=pltpu.VMEM)


def in_hbm(value):
    return pltpu.with_memory_space_constraint(value, pltpu.HBM)


def params(mib):
    return pltpu.CompilerParams(vmem_limit_bytes=mib * 1024 * 1024)


def local(strain, inv_asd, templates, tmpl_len, weights, chirp_mass, valid):
    n = lax.axis_size("bank")
    segs = lax.axis_size("seg")
    count = templates.shape[1]
    rows = strain.shape[0] // LANES
    tail_rows = OVER // LANES
    flags = valid.shape[0]
    table = {key: jnp.asarray(value) for key, value in tables(rows // 2).items()}
    tmpl_len, weights, chirp_mass, valid = map(in_hbm, (tmpl_len, weights, chirp_mass, valid))
    strain = in_hbm(strain.reshape(rows, LANES))
    asd = in_hbm(inv_asd.reshape(-1, LANES))
    tail = pl.pallas_call(
        tail_kernel,
        in_specs=[HBM] * 2,
        out_specs=VMEM,
        out_shape=pltpu.VMEM((tail_rows, LANES), F32),
        scratch_shapes=[
            pltpu.VMEM((tail_rows, LANES), F32),
            pltpu.SMEM((flags,), jnp.int32),
            pltpu.SemaphoreType.DMA((2,)),
        ],
        compiler_params=params(4),
        name="tail",
    )(valid, strain)
    halo = lax.ppermute(tail, "seg", [(i, i + 1) for i in range(segs - 1)])
    section, bank, traits = pl.pallas_call(
        early_kernel,
        in_specs=[HBM] * 7 + [VMEM],
        out_specs=[VMEM] * 3,
        out_shape=[
            pltpu.VMEM((2 * FA, FA), F32),
            pltpu.VMEM((count, 2, FA, FA), F32),
            pltpu.VMEM((trait_rows(count), LANES), F32),
        ],
        scratch_shapes=[
            pltpu.SMEM((count,), jnp.int32),
            pltpu.SMEM((count,), F32),
            pltpu.SMEM((count,), F32),
            pltpu.SMEM((flags,), jnp.int32),
            pltpu.VMEM((rows, LANES), F32),
            pltpu.VMEM((rows, LANES), F32),
            pltpu.VMEM(asd.shape, F32),
            pltpu.VMEM(table["first"].shape, BF16),
            pltpu.SemaphoreType.DMA((7,)),
        ],
        compiler_params=params(16),
        cost_estimate=pl.CostEstimate(flops=2 * 10**9, bytes_accessed=2 * 10**6, transcendentals=0),
        name="early",
    )(
        tmpl_len,
        weights,
        chirp_mass,
        valid,
        strain,
        asd,
        in_hbm(table["first"]),
        templates.astype(F32).reshape(2, count, -1, LANES),
    )
    share = rows // n
    chunk = (count * share + trait_rows(count), LANES)
    outs = pl.pallas_call(
        main_kernel,
        in_specs=[VMEM] * 10,
        out_specs=[VMEM] * n,
        out_shape=[pltpu.VMEM(chunk, F32)] * n,
        scratch_shapes=[pltpu.VMEM((count, rows, LANES), F32)],
        compiler_params=params(20),
        cost_estimate=pl.CostEstimate(flops=4 * 10**9, bytes_accessed=4 * 10**6, transcendentals=0),
        name="main",
    )(
        halo,
        section,
        bank,
        traits,
        *(table[key] for key in ("head", "second", "third", "fourth", "twist", "turn")),
    )
    banks = [outs[0]] + [
        lax.ppermute(outs[r], "bank", [(i, partner(i, r, n)) for i in range(n)]) for r in range(1, n)
    ]
    results = pl.pallas_call(
        final_kernel,
        in_specs=[VMEM] * n,
        out_specs=[VMEM] * 3,
        out_shape=[jax.ShapeDtypeStruct((share, LANES), F32)] * 3,
        compiler_params=params(8),
        name="final",
    )(*banks)
    return tuple(result.reshape(-1) for result in results)


def solution(mesh):
    placed = (P("seg"), P(), P(None, "bank", None), P("bank"), P("bank"), P("bank"), P("seg"))
    return jax.shard_map(
        local,
        mesh=mesh,
        in_specs=placed,
        out_specs=(P(("seg", "bank")), P(("seg", "bank")), P(("seg", "bank"))),
        check_vma=False,
    )
```

```python
import functools
import math

import jax
import jax.numpy as jnp
import numpy as np
from jax import lax
from jax.experimental import pallas as pl
from jax.experimental.pallas import tpu as pltpu
from jax.sharding import PartitionSpec as P

NFFT = 65536
FA = 256
HALF = 128
OVER = 16384
RATE = 4096
LANES = 128
F32 = jnp.float32
BF16 = jnp.bfloat16

TERMS = ((0, 0), (0, 1), (1, 0), (1, 1), (0, 2), (2, 0))
FEW = TERMS[:3]
PARTS = 1 + max(max(term) for term in TERMS)


def parts_of_table(table):
    rest = np.asarray(table, np.float32)
    parts = []
    for _ in range(PARTS):
        part = rest.astype(jnp.bfloat16)
        parts.append(part)
        rest = rest - part.astype(np.float32)
    return parts


def complex_rows(angle, sign):
    cos, sin = np.cos(angle), sign * np.sin(angle)
    return np.block([[cos, -sin], [sin, cos]])


def padded(rows):
    return (rows + 7) // 8 * 8


@functools.cache
def tables(hop_rows, parts_out):
    index = np.arange(FA)
    grid = index[:, None] * index[None, :]
    full = 2.0 * math.pi / FA
    first = parts_of_table(np.concatenate([np.cos(grid % FA * full), -np.sin(grid % FA * full)]))
    rows = OVER // FA
    head = np.concatenate([first[i][:, :rows] for i, _ in TERMS], axis=1)
    quarter = np.arange(FA // 4)
    second = np.concatenate(
        [
            complex_rows((2 * quarter[:, None] + odd) * index[None, :] % FA * full, -1.0).T
            for odd in range(2)
        ],
        axis=1,
    )
    second = np.concatenate([part for part in parts_of_table(second)])
    third = []
    for odd in range(2):
        angle = index[:HALF, None] * (2 * quarter[None, :] + odd) % FA * full
        parts = parts_of_table(complex_rows(angle, 1.0).T)
        third.append(np.stack(parts))
    own = hop_rows // parts_out // 2
    fourth = []
    for dest in range(parts_out):
        angle = (dest * own + np.arange(own))[:, None] * index[None, :HALF] % HALF * (2.0 * full)
        block = complex_rows(angle, 1.0).reshape(2, own, FA)
        block = np.pad(block, ((0, 0), (0, padded(own) - own), (0, 0))).reshape(-1, FA)
        fourth.append(np.stack(parts_of_table(block)[:2]))
    fine = grid * (2.0 * math.pi / NFFT)
    turn = np.repeat(index[:HALF, None] * full, LANES, axis=1)
    return {
        "first": np.stack(first),
        "head": head,
        "second": second.reshape(PARTS, 2 * FA, FA),
        "third": np.stack(third),
        "fourth": np.stack(fourth),
        "twist": np.stack([np.cos(fine), np.sin(fine)]).astype(np.float32),
        "turn": np.stack([np.cos(turn), np.sin(turn)]).astype(np.float32),
    }


def split(value, count=PARTS):
    parts = []
    for step in range(count):
        part = value.astype(BF16)
        parts.append(part)
        if step < count - 1:
            value = value - part.astype(F32)
    return parts


def dot(left, right):
    return lax.dot_general(left, right, (((1,), (0,)), ((), ())), preferred_element_type=F32)


def left_terms(parts, terms=TERMS):
    return jnp.concatenate([parts[i] for i, _ in terms], axis=1)


def right_terms(parts, terms=TERMS):
    return jnp.concatenate([parts[j] for _, j in terms], axis=0)


def log_bessel(power):
    inv = lax.rsqrt(jnp.maximum(power, 1e-30))
    rho = power * inv
    small = rho < 3.75
    t = jnp.minimum(power, 3.75 * 3.75) * (1.0 / (3.75 * 3.75))
    small_poly = 1.0 + t * (
        3.5156229
        + t * (3.0899424 + t * (1.2067492 + t * (0.2659732 + t * (0.0360768 + t * 0.0045813))))
    )
    q = jnp.minimum(3.75 * inv, 1.0)
    large_poly = 0.39894228 + q * (
        0.01328592
        + q
        * (
            0.00225319
            + q
            * (
                -0.00157565
                + q
                * (
                    0.00916281
                    + q
                    * (-0.02057706 + q * (0.02635537 + q * (-0.01647633 + q * 0.00392377)))
                )
            )
        )
    )
    inner = jnp.where(small, small_poly, large_poly * lax.rsqrt(jnp.maximum(rho, 3.75)))
    return jnp.where(small, 0.0, rho) + jnp.log(inner)


def phase(index, period):
    wrapped = ((index + period // 2) & (period - 1)) - period // 2
    angle = wrapped.astype(F32) * (2.0 * math.pi / period)
    return jnp.cos(angle), jnp.sin(angle)


def frame_of(samples):
    rows = samples.shape[0] // 2
    return jnp.concatenate([samples[pl.ds(h, rows, stride=2), :] for h in range(2)], axis=1)


def tail_kernel(
    len_hbm,
    weight_hbm,
    chirp_hbm,
    valid_hbm,
    strain_hbm,
    out_ref,
    traits_ref,
    gates_ref,
    lens,
    weights,
    chirps,
    flags,
    samples,
    sems,
):
    rows = samples.shape[0]
    blocks = flags.shape[0]
    last = strain_hbm.at[pl.ds(strain_hbm.shape[0] - rows, rows), :]
    pairs = ((last, samples), (valid_hbm, flags), (len_hbm, lens), (weight_hbm, weights), (chirp_hbm, chirps))
    copies = [pltpu.make_async_copy(a, b, sems.at[i]) for i, (a, b) in enumerate(pairs)]
    for copy in copies:
        copy.start()
    for copy in copies:
        copy.wait()
    for i in range(rows // 8):
        here = slice(8 * i, 8 * i + 8)
        out_ref[here, :] = samples[here, :] * flags[blocks - rows // 8 + i].astype(F32)
    for i in range(blocks):
        gates_ref[i : i + 1, :] = jnp.full((1, LANES), flags[i].astype(F32))
    traits_ref[...] = traits_tile(lens, weights, chirps, lens.shape[0])


def bank_kernel(traits_ref, asd_ref, tmpl_ref, bank_ref):
    count = tmpl_ref.shape[1]
    bank_ref[2 * count * FA :, :] = traits_ref[...]
    lane = lax.broadcasted_iota(jnp.int32, (1, LANES), 1)
    quarter = FA // 4
    sign = jnp.where(lane < quarter, 1.0, -1.0)
    blocks = [(q, h) for q in range(2) for h in range(2)]
    asd = {(q, h): asd_ref[pl.ds(2 * q + h, quarter, stride=4), :] for q, h in blocks}
    for k in range(count):
        delay = traits_ref[3 * k + 2 : 3 * k + 3, :LANES]
        start = OVER - (delay * RATE).astype(jnp.int32)
        energy = jnp.zeros((1, 1), F32)
        turned = {}
        for q, h in blocks:
            re = tmpl_ref[0, k, pl.ds(2 * q + h, quarter, stride=4), :] * asd[q, h]
            im = tmpl_ref[1, k, pl.ds(2 * q + h, quarter, stride=4), :] * asd[q, h]
            energy += jnp.sum(re * re + im * im, keepdims=True)
            row_cos, row_sin = phase((lane + h * LANES) * start, NFFT)
            new_re = re * row_cos + im * row_sin
            new_im = re * row_sin - im * row_cos
            turned[q, h] = (
                jnp.concatenate([new_re, new_re], axis=0).T,
                jnp.concatenate([-new_im, new_im], axis=0).T,
            )
        scale = lax.rsqrt(energy) * (1.0 / math.sqrt(NFFT))
        for q in range(2):
            col_cos, col_sin = phase((2 * (lane & (quarter - 1)) + q) * start, FA)
            col_cos, col_sin = col_cos * scale, col_sin * sign * scale
            for h in range(2):
                own, cross = turned[q, h]
                cols = slice(q * LANES, q * LANES + LANES)
                for form, value in enumerate(
                    (own * col_cos + cross * col_sin, cross * col_cos - own * col_sin)
                ):
                    first = (2 * k + form) * FA + h * HALF
                    bank_ref[first : first + HALF, cols] = value


def section_kernel(gates_ref, strain_ref, first_ref, section_ref, gated):
    for i in range(gates_ref.shape[0]):
        here = slice(8 * i, 8 * i + 8)
        gated[here, :] = strain_ref[here, :] * gates_ref[i : i + 1, :]
    frame = frame_of(gated)
    pad = jnp.zeros((FA - frame.shape[0], FA), BF16)
    frame_parts = [jnp.concatenate([pad, part], axis=0) for part in split(frame)]
    section_ref[...] = dot(left_terms([first_ref[p] for p in range(PARTS)]), right_terms(frame_parts))


def spectrum_kernel(tail_ref, section_ref, head_ref, second_ref, twist_ref, spec_ref):
    section = section_ref[...] + dot(head_ref[...], right_terms(split(frame_of(tail_ref))))
    re, im = section[:FA], section[FA:]
    turn_cos, turn_sin = twist_ref[0], twist_ref[1]
    turned = jnp.concatenate([re * turn_cos + im * turn_sin, im * turn_cos - re * turn_sin], axis=1)
    spec = dot(left_terms(split(turned)), right_terms([second_ref[p] for p in range(PARTS)]))
    spec_ref[0] = spec
    spec_ref[1] = swapped(spec)


def swapped(value):
    return jnp.concatenate(
        [pltpu.roll(value[:, i : i + LANES], LANES // 2, axis=1) for i in range(0, value.shape[1], LANES)],
        axis=1,
    )


def powers_of(spec_ref, bank_ref, k, third_ref, left, twist_ref, turn_ref):
    first = 2 * k * FA
    prod = spec_ref[0] * bank_ref[first : first + FA, :] + spec_ref[1] * bank_ref[first + FA : first + 2 * FA, :]
    even, odd = (
        dot(
            left_terms(split(prod[:, q * LANES : (q + 1) * LANES])),
            right_terms([third_ref[q, p] for p in range(PARTS)]),
        )
        for q in range(2)
    )
    plus, minus = even + odd, even - odd
    in_re = jnp.concatenate([plus[:, :HALF], minus[:, :HALF]], axis=1)
    in_im = jnp.concatenate([plus[:, HALF:], minus[:, HALF:]], axis=1)
    turn_cos, turn_sin = twist_ref[0], twist_ref[1]
    out_re = in_re * turn_cos - in_im * turn_sin
    out_im = in_re * turn_sin + in_im * turn_cos
    sum_re, sum_im = out_re[:HALF] + out_re[HALF:], out_im[:HALF] + out_im[HALF:]
    gap_re, gap_im = out_re[:HALF] - out_re[HALF:], out_im[:HALF] - out_im[HALF:]
    half_cos = jnp.concatenate([turn_ref[0]] * 2, axis=1)
    half_sin = jnp.concatenate([turn_ref[1]] * 2, axis=1)
    odd_re, odd_im = gap_re * half_cos - gap_im * half_sin, gap_re * half_sin + gap_im * half_cos
    return [
        dot(left, right_terms(split(jnp.concatenate(piece, axis=0), 2), FEW))
        for piece in ((sum_re, sum_im), (odd_re, odd_im))
    ]


def marginal(powers, traits):
    scores = [log_bessel(power) for power in powers]
    peak = functools.reduce(jnp.maximum, scores)
    masses = [weight * jnp.exp(score - peak) for score, (weight, _, _) in zip(scores, traits)]
    total = functools.reduce(jnp.add, masses)
    chirp = functools.reduce(jnp.add, [mass * trait[1] for mass, trait in zip(masses, traits)])
    delay = functools.reduce(jnp.add, [mass * trait[2] for mass, trait in zip(masses, traits)])
    inv = 1.0 / total
    return peak + jnp.log(total), chirp * inv, delay * inv


def traits_of(banks, count):
    return [
        tuple(bank[2 * count * FA + 3 * k + i : 2 * count * FA + 3 * k + i + 1, :] for i in range(3))
        for bank in banks
        for k in range(count)
    ]


def store_marginal(out_ref, powers, traits):
    rows = powers[0][0].shape[0]
    for q in range(2):
        for i, value in enumerate(marginal([power[q] for power in powers], traits)):
            first = (3 * q + i) * rows
            out_ref[first : first + rows, :] = value
    prior = functools.reduce(jnp.add, [trait[0] for trait in traits])
    out_ref[6 * rows :, :] = jnp.broadcast_to(prior, (8, FA))


def traits_tile(lens, weights, chirps, count):
    rows = trait_rows(count)
    row = lax.broadcasted_iota(jnp.int32, (rows, FA), 0)
    tile = jnp.zeros((rows, FA), F32)
    for k in range(count):
        tile = jnp.where(row == 3 * k, weights[k], tile)
        tile = jnp.where(row == 3 * k + 1, chirps[k], tile)
        tile = jnp.where(row == 3 * k + 2, lens[k].astype(F32) / RATE, tile)
    return tile


def trait_rows(count):
    return (3 * count + 7) // 8 * 8


def partner(me, r, n, group):
    return me ^ (r * group) if n & (n - 1) == 0 else (me + r * group) % n


def main_kernel(spec_ref, *refs, group):
    banks, (third_ref, fourth_ref, twist_ref, turn_ref, own_ref, *outs) = refs[:group], refs[group:]
    n = fourth_ref.shape[0]
    count = (banks[0].shape[0] - trait_rows(1)) // (2 * FA)
    me = lax.axis_index("bank")
    dests = [partner(me, r, n, group) for r in range(n // group)]
    block = fourth_ref.shape[2]
    left = left_terms(
        [jnp.concatenate([fourth_ref[dest, p] for dest in dests], axis=0) for p in range(2)], FEW
    )
    powers = []
    for bank in banks:
        for k in range(count):
            powers.append([])
            for corr in powers_of(spec_ref, bank, k, third_ref, left, twist_ref, turn_ref):
                powers[-1].append([])
                for r in range(len(dests)):
                    re = corr[r * block : r * block + block // 2]
                    im = corr[r * block + block // 2 : (r + 1) * block]
                    powers[-1][-1].append(re * re + im * im)
    traits = traits_of(banks, count)
    for r, out in enumerate(outs, 1):
        store_marginal(out, [[power[q][r] for q in range(2)] for power in powers], traits)
    for i, power in enumerate(powers):
        for q in range(2):
            own_ref[i, q] = power[q][0]


def own_kernel(power_ref, *refs):
    *banks, out_ref = refs
    powers = [[power_ref[i, q] for q in range(2)] for i in range(power_ref.shape[0])]
    store_marginal(out_ref, powers, traits_of(banks, power_ref.shape[0] // len(banks)))


def final_kernel(*refs):
    *sides, log_ref, chirp_ref, delay_ref = refs
    rows = (sides[0].shape[0] - 8) // 6
    keep = log_ref.shape[0] // 4
    prior = functools.reduce(jnp.add, [side[6 * rows : 6 * rows + 1, :] for side in sides])
    log_prior = jnp.log(prior)
    for q in range(2):
        logs, chirps, delays = (
            [side[(3 * q + i) * rows : (3 * q + i + 1) * rows, :] for side in sides] for i in range(3)
        )
        peak = functools.reduce(jnp.maximum, logs)
        masses = [jnp.exp(value - peak) for value in logs]
        total = functools.reduce(jnp.add, masses)
        inv = 1.0 / total
        chirp = functools.reduce(jnp.add, [m * value for m, value in zip(masses, chirps)]) * inv
        delay = functools.reduce(jnp.add, [m * value for m, value in zip(masses, delays)]) * inv
        level = peak + jnp.log(total) - log_prior
        for ref, value in ((log_ref, level), (chirp_ref, chirp), (delay_ref, delay)):
            for h in range(2):
                ref[pl.ds(2 * q + h, keep, stride=4), :] = value[:keep, h * LANES : (h + 1) * LANES]


HBM = pl.BlockSpec(memory_space=pltpu.HBM)
VMEM = pl.BlockSpec(memory_space=pltpu.VMEM)


def in_hbm(value):
    return pltpu.with_memory_space_constraint(value, pltpu.HBM)


def params(mib):
    return pltpu.CompilerParams(vmem_limit_bytes=mib * 1024 * 1024)


def steps(strain, inv_asd, templates, tmpl_len, weights, chirp_mass, valid):
    n = lax.axis_size("bank")
    segs = lax.axis_size("seg")
    count = templates.shape[1]
    rows = strain.shape[0] // LANES
    tail_rows = OVER // LANES
    flags = valid.shape[0]
    group = 2 if n % 2 == 0 else 1
    table = {key: jnp.asarray(value) for key, value in tables(rows // 2, n).items()}
    strain = strain.reshape(rows, LANES)
    asd = inv_asd.reshape(-1, LANES)
    tail, traits, gates = pl.pallas_call(
        tail_kernel,
        in_specs=[HBM] * 5,
        out_specs=[VMEM] * 3,
        out_shape=[
            pltpu.VMEM((tail_rows, LANES), F32),
            pltpu.VMEM((trait_rows(count), FA), F32),
            pltpu.VMEM((flags, LANES), F32),
        ],
        scratch_shapes=[
            pltpu.SMEM((count,), jnp.int32),
            pltpu.SMEM((count,), F32),
            pltpu.SMEM((count,), F32),
            pltpu.SMEM((flags,), jnp.int32),
            pltpu.VMEM((tail_rows, LANES), F32),
            pltpu.SemaphoreType.DMA((5,)),
        ],
        compiler_params=params(4),
        cost_estimate=pl.CostEstimate(flops=4 * 10**9, bytes_accessed=10**5, transcendentals=0),
        name="tail",
    )(*map(in_hbm, (tmpl_len, weights, chirp_mass, valid, strain)))
    halo = lax.ppermute(tail, "seg", [(i, i + 1) for i in range(segs - 1)])
    bank = pl.pallas_call(
        bank_kernel,
        in_specs=[VMEM] * 3,
        out_specs=VMEM,
        out_shape=pltpu.VMEM((2 * count * FA + trait_rows(count), FA), F32),
        compiler_params=params(8),
        cost_estimate=pl.CostEstimate(flops=10**6, bytes_accessed=10**4, transcendentals=0),
        name="bank",
    )(traits, asd, templates.astype(F32).reshape(2, count, -1, LANES))
    banks = [bank] + [
        lax.ppermute(bank, "bank", [(i, i // group * group + (i + r) % group) for i in range(n)])
        for r in range(1, group)
    ]
    section = pl.pallas_call(
        section_kernel,
        in_specs=[VMEM] * 3,
        out_specs=VMEM,
        out_shape=pltpu.VMEM((2 * FA, FA), F32),
        scratch_shapes=[pltpu.VMEM((rows, LANES), F32)],
        compiler_params=params(12),
        cost_estimate=pl.CostEstimate(flops=10**6, bytes_accessed=10**4, transcendentals=0),
        name="section",
    )(gates, strain, table["first"])
    spec = pl.pallas_call(
        spectrum_kernel,
        in_specs=[VMEM] * 5,
        out_specs=VMEM,
        out_shape=pltpu.VMEM((2, FA, FA), F32),
        compiler_params=params(10),
        cost_estimate=pl.CostEstimate(flops=10**6, bytes_accessed=10**4, transcendentals=0),
        name="spectrum",
    )(halo, section, table["head"], table["second"], table["twist"])
    own_rows = padded(rows // 4 // n)
    side = pltpu.VMEM((6 * own_rows + 8, FA), F32)
    powers, *outs = pl.pallas_call(
        functools.partial(main_kernel, group=group),
        in_specs=[VMEM] * (5 + group),
        out_specs=[VMEM] * (n // group),
        out_shape=[pltpu.VMEM((count * group, 2, own_rows, FA), F32)] + [side] * (n // group - 1),
        compiler_params=params(20),
        cost_estimate=pl.CostEstimate(flops=4 * 10**9, bytes_accessed=4 * 10**6, transcendentals=0),
        name="main",
    )(spec, *banks, *(table[key] for key in ("third", "fourth", "twist", "turn")))
    sides = [
        lax.ppermute(out, "bank", [(i, partner(i, r, n, group)) for i in range(n)])
        for r, out in enumerate(outs, 1)
    ]
    own = pl.pallas_call(
        own_kernel,
        in_specs=[VMEM] * (1 + group),
        out_specs=VMEM,
        out_shape=side,
        compiler_params=params(6),
        cost_estimate=pl.CostEstimate(flops=10**9, bytes_accessed=10**6, transcendentals=0),
        name="own",
    )(powers, *banks)
    results = pl.pallas_call(
        final_kernel,
        in_specs=[VMEM] * (n // group),
        out_specs=[VMEM] * 3,
        out_shape=[jax.ShapeDtypeStruct((rows // n, LANES), F32)] * 3,
        compiler_params=params(6),
        name="final",
    )(own, *sides)
    return tuple(result.reshape(-1) for result in results)


def solution(mesh):
    placed = (P("seg"), P(), P(None, "bank", None), P("bank"), P("bank"), P("bank"), P("seg"))
    return jax.shard_map(
        steps,
        mesh=mesh,
        in_specs=placed,
        out_specs=(P(("seg", "bank")), P(("seg", "bank")), P(("seg", "bank"))),
        check_vma=False,
    )
```

```python
import functools
import math

import jax
import jax.numpy as jnp
import numpy as np
from jax import lax
from jax.experimental import pallas as pl
from jax.experimental.pallas import tpu as pltpu
from jax.sharding import PartitionSpec as P

NFFT = 65536
FA = 256
HALF = 128
OVER = 16384
RATE = 4096
LANES = 128
F32 = jnp.float32
BF16 = jnp.bfloat16

TERMS = ((0, 0), (0, 1), (1, 0), (1, 1), (0, 2), (2, 0))
FEW = TERMS[:3]
PARTS = 1 + max(max(term) for term in TERMS)


def parts_of_table(table):
    rest = np.asarray(table, np.float32)
    parts = []
    for _ in range(PARTS):
        part = rest.astype(jnp.bfloat16)
        parts.append(part)
        rest = rest - part.astype(np.float32)
    return parts


def complex_rows(angle, sign):
    cos, sin = np.cos(angle), sign * np.sin(angle)
    return np.block([[cos, -sin], [sin, cos]])


def padded(rows):
    return (rows + 7) // 8 * 8


@functools.cache
def tables(hop_rows, parts_out):
    index = np.arange(FA)
    grid = index[:, None] * index[None, :]
    full = 2.0 * math.pi / FA
    first = parts_of_table(np.concatenate([np.cos(grid % FA * full), -np.sin(grid % FA * full)]))
    rows = OVER // FA
    head = np.concatenate([first[i][:, :rows] for i, _ in TERMS], axis=1)
    quarter = np.arange(FA // 4)
    second = np.concatenate(
        [
            complex_rows((2 * quarter[:, None] + odd) * index[None, :] % FA * full, -1.0).T
            for odd in range(2)
        ],
        axis=1,
    )
    second = np.concatenate([part for part in parts_of_table(second)])
    third = []
    for odd in range(2):
        angle = index[:HALF, None] * (2 * quarter[None, :] + odd) % FA * full
        parts = parts_of_table(complex_rows(angle, 1.0).T)
        third.append(np.stack(parts))
    own = hop_rows // parts_out // 2
    fourth = []
    for dest in range(parts_out):
        angle = (dest * own + np.arange(own))[:, None] * index[None, :HALF] % HALF * (2.0 * full)
        block = complex_rows(angle, 1.0).reshape(2, own, FA)
        block = np.pad(block, ((0, 0), (0, padded(own) - own), (0, 0))).reshape(-1, FA)
        fourth.append(np.stack(parts_of_table(block)[:2]))
    fine = grid * (2.0 * math.pi / NFFT)
    turn = np.repeat(index[:HALF, None] * full, LANES, axis=1)
    return {
        "first": np.stack(first),
        "head": head,
        "second": second.reshape(PARTS, 2 * FA, FA),
        "third": np.stack(third),
        "fourth": np.stack(fourth),
        "twist": np.stack([np.cos(fine), np.sin(fine)]).astype(np.float32),
        "turn": np.stack([np.cos(turn), np.sin(turn)]).astype(np.float32),
    }


def split(value, count=PARTS):
    parts = []
    for step in range(count):
        part = value.astype(BF16)
        parts.append(part)
        if step < count - 1:
            value = value - part.astype(F32)
    return parts


def dot(left, right):
    return lax.dot_general(left, right, (((1,), (0,)), ((), ())), preferred_element_type=F32)


def left_terms(parts, terms=TERMS):
    return jnp.concatenate([parts[i] for i, _ in terms], axis=1)


def right_terms(parts, terms=TERMS):
    return jnp.concatenate([parts[j] for _, j in terms], axis=0)


def log_bessel(power):
    inv = lax.rsqrt(jnp.maximum(power, 1e-30))
    rho = power * inv
    small = rho < 3.75
    t = jnp.minimum(power, 3.75 * 3.75) * (1.0 / (3.75 * 3.75))
    small_poly = 1.0 + t * (
        3.5156229
        + t * (3.0899424 + t * (1.2067492 + t * (0.2659732 + t * (0.0360768 + t * 0.0045813))))
    )
    q = jnp.minimum(3.75 * inv, 1.0)
    large_poly = 0.39894228 + q * (
        0.01328592
        + q
        * (
            0.00225319
            + q
            * (
                -0.00157565
                + q
                * (
                    0.00916281
                    + q
                    * (-0.02057706 + q * (0.02635537 + q * (-0.01647633 + q * 0.00392377)))
                )
            )
        )
    )
    inner = jnp.where(small, small_poly, large_poly * lax.rsqrt(jnp.maximum(rho, 3.75)))
    return jnp.where(small, 0.0, rho) + jnp.log(inner)


def phase(index, period):
    wrapped = ((index + period // 2) & (period - 1)) - period // 2
    angle = wrapped.astype(F32) * (2.0 * math.pi / period)
    return jnp.cos(angle), jnp.sin(angle)


def frame_of(samples):
    rows = samples.shape[0] // 2
    return jnp.concatenate([samples[pl.ds(h, rows, stride=2), :] for h in range(2)], axis=1)


def tail_kernel(
    len_hbm,
    weight_hbm,
    chirp_hbm,
    valid_hbm,
    strain_hbm,
    out_ref,
    traits_ref,
    gates_ref,
    lens,
    weights,
    chirps,
    flags,
    samples,
    sems,
):
    rows = samples.shape[0]
    blocks = flags.shape[0]
    last = strain_hbm.at[pl.ds(strain_hbm.shape[0] - rows, rows), :]
    pairs = ((last, samples), (valid_hbm, flags), (len_hbm, lens), (weight_hbm, weights), (chirp_hbm, chirps))
    copies = [pltpu.make_async_copy(a, b, sems.at[i]) for i, (a, b) in enumerate(pairs)]
    for copy in copies:
        copy.start()
    for copy in copies:
        copy.wait()
    for i in range(rows // 8):
        here = slice(8 * i, 8 * i + 8)
        out_ref[here, :] = samples[here, :] * flags[blocks - rows // 8 + i].astype(F32)
    for i in range(blocks):
        gates_ref[i : i + 1, :] = jnp.full((1, LANES), flags[i].astype(F32))
    traits_ref[...] = traits_tile(lens, weights, chirps, lens.shape[0])


def bank_kernel(traits_ref, asd_ref, tmpl_ref, bank_ref):
    count = tmpl_ref.shape[1]
    bank_ref[2 * count * FA :, :] = traits_ref[...]
    lane = lax.broadcasted_iota(jnp.int32, (1, LANES), 1)
    quarter = FA // 4
    sign = jnp.where(lane < quarter, 1.0, -1.0)
    blocks = [(q, h) for q in range(2) for h in range(2)]
    asd = {(q, h): asd_ref[pl.ds(2 * q + h, quarter, stride=4), :] for q, h in blocks}
    for k in range(count):
        delay = traits_ref[3 * k + 2 : 3 * k + 3, :LANES]
        start = OVER - (delay * RATE).astype(jnp.int32)
        energy = jnp.zeros((1, 1), F32)
        turned = {}
        for q, h in blocks:
            re = tmpl_ref[0, k, pl.ds(2 * q + h, quarter, stride=4), :] * asd[q, h]
            im = tmpl_ref[1, k, pl.ds(2 * q + h, quarter, stride=4), :] * asd[q, h]
            energy += jnp.sum(re * re + im * im, keepdims=True)
            row_cos, row_sin = phase((lane + h * LANES) * start, NFFT)
            new_re = re * row_cos + im * row_sin
            new_im = re * row_sin - im * row_cos
            turned[q, h] = (
                jnp.concatenate([new_re, new_re], axis=0).T,
                jnp.concatenate([-new_im, new_im], axis=0).T,
            )
        scale = lax.rsqrt(energy) * (1.0 / math.sqrt(NFFT))
        for q in range(2):
            col_cos, col_sin = phase((2 * (lane & (quarter - 1)) + q) * start, FA)
            col_cos, col_sin = col_cos * scale, col_sin * sign * scale
            for h in range(2):
                own, cross = turned[q, h]
                cols = slice(q * LANES, q * LANES + LANES)
                for form, value in enumerate(
                    (own * col_cos + cross * col_sin, cross * col_cos - own * col_sin)
                ):
                    first = (2 * k + form) * FA + h * HALF
                    bank_ref[first : first + HALF, cols] = value


def section_kernel(gates_ref, strain_ref, first_ref, section_ref, gated):
    for i in range(gates_ref.shape[0]):
        here = slice(8 * i, 8 * i + 8)
        gated[here, :] = strain_ref[here, :] * gates_ref[i : i + 1, :]
    frame = frame_of(gated)
    pad = jnp.zeros((FA - frame.shape[0], FA), BF16)
    frame_parts = [jnp.concatenate([pad, part], axis=0) for part in split(frame)]
    section_ref[...] = dot(left_terms([first_ref[p] for p in range(PARTS)]), right_terms(frame_parts))


def spectrum_kernel(section_ref, head_ref, second_ref, twist_ref, *refs, segs):
    *halos, spec_ref = refs
    seg = lax.axis_index("seg")
    halo = frame_of(halos[0])
    if len(halos) > 1:
        halo = jnp.where(seg == segs // 2 - 1, frame_of(halos[1]), halo)
    halo = jnp.where(seg == 0, 0.0, halo)
    section = section_ref[...] + dot(head_ref[...], right_terms(split(halo)))
    re, im = section[:FA], section[FA:]
    turn_cos, turn_sin = twist_ref[0], twist_ref[1]
    turned = jnp.concatenate([re * turn_cos + im * turn_sin, im * turn_cos - re * turn_sin], axis=1)
    spec = dot(left_terms(split(turned)), right_terms([second_ref[p] for p in range(PARTS)]))
    spec_ref[0] = spec
    spec_ref[1] = swapped(spec)


def swapped(value):
    return jnp.concatenate(
        [pltpu.roll(value[:, i : i + LANES], LANES // 2, axis=1) for i in range(0, value.shape[1], LANES)],
        axis=1,
    )


def powers_of(spec_ref, bank_ref, k, third_ref, left, twist_ref, turn_ref):
    first = 2 * k * FA
    prod = spec_ref[0] * bank_ref[first : first + FA, :] + spec_ref[1] * bank_ref[first + FA : first + 2 * FA, :]
    even, odd = (
        dot(
            left_terms(split(prod[:, q * LANES : (q + 1) * LANES])),
            right_terms([third_ref[q, p] for p in range(PARTS)]),
        )
        for q in range(2)
    )
    plus, minus = even + odd, even - odd
    in_re = jnp.concatenate([plus[:, :HALF], minus[:, :HALF]], axis=1)
    in_im = jnp.concatenate([plus[:, HALF:], minus[:, HALF:]], axis=1)
    turn_cos, turn_sin = twist_ref[0], twist_ref[1]
    out_re = in_re * turn_cos - in_im * turn_sin
    out_im = in_re * turn_sin + in_im * turn_cos
    sum_re, sum_im = out_re[:HALF] + out_re[HALF:], out_im[:HALF] + out_im[HALF:]
    gap_re, gap_im = out_re[:HALF] - out_re[HALF:], out_im[:HALF] - out_im[HALF:]
    half_cos = jnp.concatenate([turn_ref[0]] * 2, axis=1)
    half_sin = jnp.concatenate([turn_ref[1]] * 2, axis=1)
    odd_re, odd_im = gap_re * half_cos - gap_im * half_sin, gap_re * half_sin + gap_im * half_cos
    return [
        dot(left, right_terms(split(jnp.concatenate(piece, axis=0), 2), FEW))
        for piece in ((sum_re, sum_im), (odd_re, odd_im))
    ]


def marginal(powers, traits):
    scores = [log_bessel(power) for power in powers]
    peak = functools.reduce(jnp.maximum, scores)
    masses = [weight * jnp.exp(score - peak) for score, (weight, _, _) in zip(scores, traits)]
    total = functools.reduce(jnp.add, masses)
    chirp = functools.reduce(jnp.add, [mass * trait[1] for mass, trait in zip(masses, traits)])
    delay = functools.reduce(jnp.add, [mass * trait[2] for mass, trait in zip(masses, traits)])
    inv = 1.0 / total
    return peak + jnp.log(total), chirp * inv, delay * inv


def traits_of(banks, count):
    return [
        tuple(bank[2 * count * FA + 3 * k + i : 2 * count * FA + 3 * k + i + 1, :] for i in range(3))
        for bank in banks
        for k in range(count)
    ]


def store_marginal(out_ref, powers, traits):
    rows = powers[0][0].shape[0]
    for q in range(2):
        for i, value in enumerate(marginal([power[q] for power in powers], traits)):
            first = (3 * q + i) * rows
            out_ref[first : first + rows, :] = value
    prior = functools.reduce(jnp.add, [trait[0] for trait in traits])
    out_ref[6 * rows :, :] = jnp.broadcast_to(prior, (8, FA))


def traits_tile(lens, weights, chirps, count):
    rows = trait_rows(count)
    row = lax.broadcasted_iota(jnp.int32, (rows, FA), 0)
    tile = jnp.zeros((rows, FA), F32)
    for k in range(count):
        tile = jnp.where(row == 3 * k, weights[k], tile)
        tile = jnp.where(row == 3 * k + 1, chirps[k], tile)
        tile = jnp.where(row == 3 * k + 2, lens[k].astype(F32) / RATE, tile)
    return tile


def trait_rows(count):
    return (3 * count + 7) // 8 * 8


def partner(me, r, n, group):
    return me ^ (r * group) if n & (n - 1) == 0 else (me + r * group) % n


def main_kernel(spec_ref, *refs, group):
    banks, (third_ref, fourth_ref, twist_ref, turn_ref, own_ref, *outs) = refs[:group], refs[group:]
    n = fourth_ref.shape[0]
    count = (banks[0].shape[0] - trait_rows(1)) // (2 * FA)
    me = lax.axis_index("bank")
    dests = [partner(me, r, n, group) for r in range(n // group)]
    block = fourth_ref.shape[2]
    left = left_terms(
        [jnp.concatenate([fourth_ref[dest, p] for dest in dests], axis=0) for p in range(2)], FEW
    )
    powers = []
    for bank in banks:
        for k in range(count):
            powers.append([])
            for corr in powers_of(spec_ref, bank, k, third_ref, left, twist_ref, turn_ref):
                powers[-1].append([])
                for r in range(len(dests)):
                    re = corr[r * block : r * block + block // 2]
                    im = corr[r * block + block // 2 : (r + 1) * block]
                    powers[-1][-1].append(re * re + im * im)
    traits = traits_of(banks, count)
    for r, out in enumerate(outs, 1):
        store_marginal(out, [[power[q][r] for q in range(2)] for power in powers], traits)
    for i, power in enumerate(powers):
        for q in range(2):
            own_ref[i, q] = power[q][0]


def own_kernel(power_ref, *refs):
    *banks, out_ref = refs
    powers = [[power_ref[i, q] for q in range(2)] for i in range(power_ref.shape[0])]
    store_marginal(out_ref, powers, traits_of(banks, power_ref.shape[0] // len(banks)))


def final_kernel(*refs):
    *sides, log_ref, chirp_ref, delay_ref = refs
    rows = (sides[0].shape[0] - 8) // 6
    keep = log_ref.shape[0] // 4
    prior = functools.reduce(jnp.add, [side[6 * rows : 6 * rows + 1, :] for side in sides])
    log_prior = jnp.log(prior)
    for q in range(2):
        logs, chirps, delays = (
            [side[(3 * q + i) * rows : (3 * q + i + 1) * rows, :] for side in sides] for i in range(3)
        )
        peak = functools.reduce(jnp.maximum, logs)
        masses = [jnp.exp(value - peak) for value in logs]
        total = functools.reduce(jnp.add, masses)
        inv = 1.0 / total
        chirp = functools.reduce(jnp.add, [m * value for m, value in zip(masses, chirps)]) * inv
        delay = functools.reduce(jnp.add, [m * value for m, value in zip(masses, delays)]) * inv
        level = peak + jnp.log(total) - log_prior
        for ref, value in ((log_ref, level), (chirp_ref, chirp), (delay_ref, delay)):
            for h in range(2):
                ref[pl.ds(2 * q + h, keep, stride=4), :] = value[:keep, h * LANES : (h + 1) * LANES]


HBM = pl.BlockSpec(memory_space=pltpu.HBM)
VMEM = pl.BlockSpec(memory_space=pltpu.VMEM)


def in_hbm(value):
    return pltpu.with_memory_space_constraint(value, pltpu.HBM)


def params(mib):
    return pltpu.CompilerParams(vmem_limit_bytes=mib * 1024 * 1024)


def halo_routes(segs, n):
    cut = segs // 2 - 1
    if n % 2 or cut < 2:
        return [(i, i + 1) for i in range(segs - 1)], []
    closing = {cut - 1: 0, segs - 1: cut}
    ring = [(i, closing.get(i, i + 1)) for i in range(segs)]
    bridge = []
    for i in range(segs):
        for j in range(n):
            to = (2 * cut - 1 - i) * n + j if i in (cut - 1, cut) else i * n + (j ^ 1)
            bridge.append((i * n + j, to))
    return ring, bridge


def steps(strain, inv_asd, templates, tmpl_len, weights, chirp_mass, valid):
    n = lax.axis_size("bank")
    segs = lax.axis_size("seg")
    count = templates.shape[1]
    rows = strain.shape[0] // LANES
    tail_rows = OVER // LANES
    flags = valid.shape[0]
    group = 2 if n % 2 == 0 else 1
    table = {key: jnp.asarray(value) for key, value in tables(rows // 2, n).items()}
    strain = strain.reshape(rows, LANES)
    asd = inv_asd.reshape(-1, LANES)
    tail, traits, gates = pl.pallas_call(
        tail_kernel,
        in_specs=[HBM] * 5,
        out_specs=[VMEM] * 3,
        out_shape=[
            pltpu.VMEM((tail_rows, LANES), F32),
            pltpu.VMEM((trait_rows(count), FA), F32),
            pltpu.VMEM((flags, LANES), F32),
        ],
        scratch_shapes=[
            pltpu.SMEM((count,), jnp.int32),
            pltpu.SMEM((count,), F32),
            pltpu.SMEM((count,), F32),
            pltpu.SMEM((flags,), jnp.int32),
            pltpu.VMEM((tail_rows, LANES), F32),
            pltpu.SemaphoreType.DMA((5,)),
        ],
        compiler_params=params(4),
        cost_estimate=pl.CostEstimate(flops=4 * 10**9, bytes_accessed=10**5, transcendentals=0),
        name="tail",
    )(*map(in_hbm, (tmpl_len, weights, chirp_mass, valid, strain)))
    ring, bridge = halo_routes(segs, n)
    halos = [lax.ppermute(tail, "seg", ring)]
    if bridge:
        halos.append(lax.ppermute(tail, ("seg", "bank"), bridge))
    bank = pl.pallas_call(
        bank_kernel,
        in_specs=[VMEM] * 3,
        out_specs=VMEM,
        out_shape=pltpu.VMEM((2 * count * FA + trait_rows(count), FA), F32),
        compiler_params=params(8),
        cost_estimate=pl.CostEstimate(flops=10**6, bytes_accessed=10**4, transcendentals=0),
        name="bank",
    )(traits, asd, templates.astype(F32).reshape(2, count, -1, LANES))
    banks = [bank] + [
        lax.ppermute(bank, "bank", [(i, i // group * group + (i + r) % group) for i in range(n)])
        for r in range(1, group)
    ]
    section = pl.pallas_call(
        section_kernel,
        in_specs=[VMEM] * 3,
        out_specs=VMEM,
        out_shape=pltpu.VMEM((2 * FA, FA), F32),
        scratch_shapes=[pltpu.VMEM((rows, LANES), F32)],
        compiler_params=params(12),
        cost_estimate=pl.CostEstimate(flops=10**6, bytes_accessed=10**4, transcendentals=0),
        name="section",
    )(gates, strain, table["first"])
    spec = pl.pallas_call(
        functools.partial(spectrum_kernel, segs=segs),
        in_specs=[VMEM] * (4 + len(halos)),
        out_specs=VMEM,
        out_shape=pltpu.VMEM((2, FA, FA), F32),
        compiler_params=params(10),
        cost_estimate=pl.CostEstimate(flops=10**6, bytes_accessed=10**4, transcendentals=0),
        name="spectrum",
    )(section, table["head"], table["second"], table["twist"], *halos)
    own_rows = padded(rows // 4 // n)
    side = pltpu.VMEM((6 * own_rows + 8, FA), F32)
    powers, *outs = pl.pallas_call(
        functools.partial(main_kernel, group=group),
        in_specs=[VMEM] * (5 + group),
        out_specs=[VMEM] * (n // group),
        out_shape=[pltpu.VMEM((count * group, 2, own_rows, FA), F32)] + [side] * (n // group - 1),
        compiler_params=params(20),
        cost_estimate=pl.CostEstimate(flops=4 * 10**9, bytes_accessed=4 * 10**6, transcendentals=0),
        name="main",
    )(spec, *banks, *(table[key] for key in ("third", "fourth", "twist", "turn")))
    sides = [
        lax.ppermute(out, "bank", [(i, partner(i, r, n, group)) for i in range(n)])
        for r, out in enumerate(outs, 1)
    ]
    own = pl.pallas_call(
        own_kernel,
        in_specs=[VMEM] * (1 + group),
        out_specs=VMEM,
        out_shape=side,
        compiler_params=params(6),
        cost_estimate=pl.CostEstimate(flops=10**9, bytes_accessed=10**6, transcendentals=0),
        name="own",
    )(powers, *banks)
    results = pl.pallas_call(
        final_kernel,
        in_specs=[VMEM] * (n // group),
        out_specs=[VMEM] * 3,
        out_shape=[jax.ShapeDtypeStruct((rows // n, LANES), F32)] * 3,
        compiler_params=params(6),
        name="final",
    )(own, *sides)
    return tuple(result.reshape(-1) for result in results)


def solution(mesh):
    placed = (P("seg"), P(), P(None, "bank", None), P("bank"), P("bank"), P("bank"), P("seg"))
    return jax.shard_map(
        steps,
        mesh=mesh,
        in_specs=placed,
        out_specs=(P(("seg", "bank")), P(("seg", "bank")), P(("seg", "bank"))),
        check_vma=False,
    )
```

```python
import functools
import math

import jax
import jax.numpy as jnp
import numpy as np
from jax import lax
from jax.experimental import pallas as pl
from jax.experimental.pallas import tpu as pltpu
from jax.sharding import PartitionSpec as P

NFFT = 65536
FA = 256
HALF = 128
OVER = 16384
RATE = 4096
LANES = 128
F32 = jnp.float32
BF16 = jnp.bfloat16

TERMS = ((0, 0), (0, 1), (1, 0), (1, 1), (0, 2), (2, 0))
FEW = TERMS[:3]
MOST = TERMS[:5]
PARTS = 1 + max(max(term) for term in TERMS)


def parts_of_table(table):
    rest = np.asarray(table, np.float32)
    parts = []
    for _ in range(PARTS):
        part = rest.astype(jnp.bfloat16)
        parts.append(part)
        rest = rest - part.astype(np.float32)
    return parts


def complex_rows(angle, sign):
    cos, sin = np.cos(angle), sign * np.sin(angle)
    return np.block([[cos, -sin], [sin, cos]])


def padded(rows):
    return (rows + 7) // 8 * 8


@functools.cache
def tables(hop_rows, parts_out):
    index = np.arange(FA)
    grid = index[:, None] * index[None, :]
    full = 2.0 * math.pi / FA
    first = parts_of_table(np.concatenate([np.cos(grid % FA * full), -np.sin(grid % FA * full)]))
    rows = OVER // FA
    head = np.concatenate([first[i][:, :rows] for i, _ in TERMS], axis=1)
    quarter = np.arange(FA // 4)
    second = np.concatenate(
        [
            complex_rows((2 * quarter[:, None] + odd) * index[None, :] % FA * full, -1.0).T
            for odd in range(2)
        ],
        axis=1,
    )
    second = np.concatenate([part for part in parts_of_table(second)])
    third = []
    for odd in range(2):
        angle = index[:HALF, None] * (2 * quarter[None, :] + odd) % FA * full
        parts = parts_of_table(complex_rows(angle, 1.0).T)
        third.append(np.stack(parts))
    own = hop_rows // parts_out // 2
    fourth = np.zeros((parts_out, 2, 2, 2 * padded(own), FA), jnp.bfloat16)
    for dest in range(parts_out):
        for odd in range(2):
            row = 2 * (dest * own + np.arange(own)) + odd
            block = complex_rows(row[:, None] * index[None, :HALF] % FA * full, 1.0).reshape(2, own, FA)
            block = np.pad(block, ((0, 0), (0, padded(own) - own), (0, 0))).reshape(-1, FA)
            fourth[dest, odd] = np.stack(parts_of_table(block)[:2])
    fine = grid * (2.0 * math.pi / NFFT)
    return {
        "first": np.stack(first),
        "head": head,
        "second": second.reshape(PARTS, 2 * FA, FA),
        "third": np.stack(third),
        "fourth": fourth,
        "twist": np.stack([np.cos(fine), np.sin(fine)]).astype(np.float32),
    }


def split(value, count=PARTS):
    parts = []
    for step in range(count):
        part = value.astype(BF16)
        parts.append(part)
        if step < count - 1:
            value = value - part.astype(F32)
    return parts


def dot(left, right):
    return lax.dot_general(left, right, (((1,), (0,)), ((), ())), preferred_element_type=F32)


def left_terms(parts, terms=TERMS):
    return jnp.concatenate([parts[i] for i, _ in terms], axis=1)


def right_terms(parts, terms=TERMS):
    return jnp.concatenate([parts[j] for _, j in terms], axis=0)


SMALL = [1.0, 3.5156229, 3.0899424, 1.2067492, 0.2659732, 0.0360768, 0.0045813]
LARGE = [
    0.39894228,
    0.01328592,
    0.00225319,
    -0.00157565,
    0.00916281,
    -0.02057706,
    0.02635537,
    -0.01647633,
    0.00392377,
]
EDGE = 3.75


def polynomial(coefficients, value):
    total = coefficients[-1]
    for coefficient in coefficients[-2::-1]:
        total = coefficient + value * total
    return total


def log_bessel(power):
    inv = lax.rsqrt(power)
    rho = power * inv
    small = power < EDGE * EDGE
    small_poly = polynomial([c / EDGE ** (2 * i) for i, c in enumerate(SMALL)], power)
    large_poly = polynomial([c * EDGE**i for i, c in enumerate(LARGE)], inv)
    inner = jnp.where(small, small_poly, large_poly * lax.rsqrt(rho))
    return jnp.where(small, 0.0, rho) + jnp.log(inner)


def phase(index, period):
    wrapped = ((index + period // 2) & (period - 1)) - period // 2
    angle = wrapped.astype(F32) * (2.0 * math.pi / period)
    return jnp.cos(angle), jnp.sin(angle)


def frame_of(samples):
    rows = samples.shape[0] // 2
    return jnp.concatenate([samples[pl.ds(h, rows, stride=2), :] for h in range(2)], axis=1)


def tail_kernel(
    len_hbm,
    weight_hbm,
    chirp_hbm,
    valid_hbm,
    strain_hbm,
    out_ref,
    traits_ref,
    gates_ref,
    lens,
    weights,
    chirps,
    flags,
    samples,
    sems,
):
    rows = samples.shape[0]
    blocks = flags.shape[0]
    last = strain_hbm.at[pl.ds(strain_hbm.shape[0] - rows, rows), :]
    pairs = ((last, samples), (valid_hbm, flags), (len_hbm, lens), (weight_hbm, weights), (chirp_hbm, chirps))
    copies = [pltpu.make_async_copy(a, b, sems.at[i]) for i, (a, b) in enumerate(pairs)]
    for copy in copies:
        copy.start()
    for copy in copies:
        copy.wait()
    for i in range(rows // 8):
        here = slice(8 * i, 8 * i + 8)
        out_ref[here, :] = samples[here, :] * flags[blocks - rows // 8 + i].astype(F32)
    for i in range(blocks):
        gates_ref[i : i + 1, :] = jnp.full((1, LANES), flags[i].astype(F32))
    traits_ref[...] = traits_tile(lens, weights, chirps, lens.shape[0])


def bank_kernel(traits_ref, asd_ref, tmpl_ref, bank_ref):
    count = tmpl_ref.shape[1]
    bank_ref[2 * count * FA :, :] = traits_ref[...]
    lane = lax.broadcasted_iota(jnp.int32, (1, LANES), 1)
    quarter = FA // 4
    sign = jnp.where(lane < quarter, 1.0, -1.0)
    blocks = [(q, h) for q in range(2) for h in range(2)]
    asd = {(q, h): asd_ref[pl.ds(2 * q + h, quarter, stride=4), :] for q, h in blocks}
    for k in range(count):
        delay = traits_ref[3 * k + 2 : 3 * k + 3, :LANES]
        start = OVER - (delay * RATE).astype(jnp.int32)
        energy = jnp.zeros((1, 1), F32)
        turned = {}
        for q, h in blocks:
            re = tmpl_ref[0, k, pl.ds(2 * q + h, quarter, stride=4), :] * asd[q, h]
            im = tmpl_ref[1, k, pl.ds(2 * q + h, quarter, stride=4), :] * asd[q, h]
            energy += jnp.sum(re * re + im * im, keepdims=True)
            row_cos, row_sin = phase((lane + h * LANES) * start, NFFT)
            new_re = re * row_cos + im * row_sin
            new_im = re * row_sin - im * row_cos
            turned[q, h] = (
                jnp.concatenate([new_re, new_re], axis=0).T,
                jnp.concatenate([-new_im, new_im], axis=0).T,
            )
        scale = lax.rsqrt(energy) * (1.0 / math.sqrt(NFFT))
        for q in range(2):
            col_cos, col_sin = phase((2 * (lane & (quarter - 1)) + q) * start, FA)
            col_cos, col_sin = col_cos * scale, col_sin * sign * scale
            for h in range(2):
                own, cross = turned[q, h]
                cols = slice(q * LANES, q * LANES + LANES)
                for form, value in enumerate(
                    (own * col_cos + cross * col_sin, cross * col_cos - own * col_sin)
                ):
                    first = (2 * k + form) * FA + h * HALF
                    bank_ref[first : first + HALF, cols] = value


def section_kernel(gates_ref, strain_ref, first_ref, section_ref, gated):
    for i in range(gates_ref.shape[0]):
        here = slice(8 * i, 8 * i + 8)
        gated[here, :] = strain_ref[here, :] * gates_ref[i : i + 1, :]
    frame = frame_of(gated)
    pad = jnp.zeros((FA - frame.shape[0], FA), BF16)
    frame_parts = [jnp.concatenate([pad, part], axis=0) for part in split(frame)]
    section_ref[...] = dot(left_terms([first_ref[p] for p in range(PARTS)]), right_terms(frame_parts))


def spectrum_kernel(section_ref, head_ref, second_ref, twist_ref, *refs, segs):
    *halos, spec_ref = refs
    seg = lax.axis_index("seg")
    halo = frame_of(halos[0])
    if len(halos) > 1:
        halo = jnp.where(seg == segs // 2 - 1, frame_of(halos[1]), halo)
    halo = jnp.where(seg == 0, 0.0, halo)
    halo_terms = right_terms(split(halo))
    second = right_terms([second_ref[p] for p in range(PARTS)])
    size = FA // 2
    sections = []
    for r in range(0, FA, size):
        both = jnp.concatenate([head_ref[r : r + size, :], head_ref[FA + r : FA + r + size, :]], axis=0)
        sections.append(dot(both, halo_terms))
    for i, extra in enumerate(sections):
        here = slice(i * size, (i + 1) * size)
        re = section_ref[here, :] + extra[:size]
        im = section_ref[FA + i * size : FA + (i + 1) * size, :] + extra[size:]
        turn_cos, turn_sin = twist_ref[0, here, :], twist_ref[1, here, :]
        turned = jnp.concatenate([re * turn_cos + im * turn_sin, im * turn_cos - re * turn_sin], axis=1)
        spec = dot(left_terms(split(turned)), second)
        spec_ref[0, here, :] = spec
        spec_ref[1, here, :] = swapped(spec)


def swapped(value):
    return jnp.concatenate(
        [pltpu.roll(value[:, i : i + LANES], LANES // 2, axis=1) for i in range(0, value.shape[1], LANES)],
        axis=1,
    )


ROWS = 32


def product_terms(spec_ref, bank_ref, k):
    first = 2 * k * FA
    parts = [[], []]
    for r in range(0, FA, ROWS):
        here = slice(r, r + ROWS)
        prod = (
            spec_ref[0, here, :] * bank_ref[first + r : first + r + ROWS, :]
            + spec_ref[1, here, :] * bank_ref[first + FA + r : first + FA + r + ROWS, :]
        )
        for q in range(2):
            parts[q].append(left_terms(split(prod[:, q * LANES : (q + 1) * LANES], 2), MOST))
    return [jnp.concatenate(part, axis=0) for part in parts]


def last_terms(even, odd, twist_ref):
    parts = [[[], []] for _ in range(4)]
    for r in range(0, HALF, ROWS):
        turned = []
        for here in (slice(r, r + ROWS), slice(HALF + r, HALF + r + ROWS)):
            plus, minus = even[here] + odd[here], even[here] - odd[here]
            in_re = jnp.concatenate([plus[:, :HALF], minus[:, :HALF]], axis=1)
            in_im = jnp.concatenate([plus[:, HALF:], minus[:, HALF:]], axis=1)
            turn_cos, turn_sin = twist_ref[0, here, :], twist_ref[1, here, :]
            turned.append(
                (in_re * turn_cos - in_im * turn_sin, in_re * turn_sin + in_im * turn_cos)
            )
        (low_re, low_im), (high_re, high_im) = turned
        values = (low_re + high_re, low_im + high_im, low_re - high_re, low_im - high_im)
        for part, value in zip(parts, values):
            for p, piece in enumerate(split(value, 2)):
                part[p].append(piece)
    return [
        right_terms([jnp.concatenate(parts[2 * q][p] + parts[2 * q + 1][p], axis=0) for p in range(2)], FEW)
        for q in range(2)
    ]


def marginal(scores, traits):
    peak = functools.reduce(jnp.maximum, scores)
    masses = [weight * jnp.exp(score - peak) for score, (weight, _, _) in zip(scores, traits)]
    total = functools.reduce(jnp.add, masses)
    chirp = functools.reduce(jnp.add, [mass * trait[1] for mass, trait in zip(masses, traits)])
    delay = functools.reduce(jnp.add, [mass * trait[2] for mass, trait in zip(masses, traits)])
    inv = 1.0 / total
    return peak + jnp.log(total), chirp * inv, delay * inv


def traits_of(banks, count):
    return [
        tuple(bank[2 * count * FA + 3 * k + i : 2 * count * FA + 3 * k + i + 1, :] for i in range(3))
        for bank in banks
        for k in range(count)
    ]


def store_marginal(out_ref, scores, traits):
    rows = scores[0][0].shape[0]
    for q in range(2):
        for i, value in enumerate(marginal([score[q] for score in scores], traits)):
            first = (3 * q + i) * rows
            out_ref[first : first + rows, :] = value
    prior = functools.reduce(jnp.add, [trait[0] for trait in traits])
    out_ref[6 * rows :, :] = jnp.broadcast_to(prior, (8, FA))


def traits_tile(lens, weights, chirps, count):
    rows = trait_rows(count)
    row = lax.broadcasted_iota(jnp.int32, (rows, FA), 0)
    tile = jnp.zeros((rows, FA), F32)
    for k in range(count):
        tile = jnp.where(row == 3 * k, weights[k], tile)
        tile = jnp.where(row == 3 * k + 1, chirps[k], tile)
        tile = jnp.where(row == 3 * k + 2, lens[k].astype(F32) / RATE, tile)
    return tile


def trait_rows(count):
    return (3 * count + 7) // 8 * 8


def partner(me, r, n, group):
    return me ^ (r * group) if n & (n - 1) == 0 else (me + r * group) % n


def main_kernel(spec_ref, *refs, group):
    banks, (third_ref, fourth_ref, twist_ref, own_ref, *outs) = refs[:group], refs[group:]
    n = fourth_ref.shape[0]
    count = (banks[0].shape[0] - trait_rows(1)) // (2 * FA)
    me = lax.axis_index("bank")
    dests = [partner(me, r, n, group) for r in range(n // group)]
    block = fourth_ref.shape[3]
    lefts = [
        left_terms(
            [jnp.concatenate([fourth_ref[dest, q, p] for dest in dests], axis=0) for p in range(2)], FEW
        )
        for q in range(2)
    ]
    third = [right_terms([third_ref[q, p] for p in range(PARTS)], MOST) for q in range(2)]
    work = [(bank, k) for bank in banks for k in range(count)]

    def sums(bank, k):
        terms = product_terms(spec_ref, bank, k)
        return [dot(terms[q], third[q]) for q in range(2)]

    scores = []
    ready = sums(*work[0])
    for i in range(len(work)):
        now, ready = ready, sums(*work[i + 1]) if i + 1 < len(work) else None
        scores.append([[] for _ in outs])
        for q, piece in enumerate(last_terms(*now, twist_ref)):
            corr = dot(lefts[q], piece)
            for r in range(len(dests)):
                re = corr[r * block : r * block + block // 2]
                im = corr[r * block + block // 2 : (r + 1) * block]
                if r:
                    scores[i][r - 1].append(log_bessel(re * re + im * im))
                else:
                    own_ref[i, q] = re * re + im * im
    traits = traits_of(banks, count)
    for r, out in enumerate(outs):
        store_marginal(out, [score[r] for score in scores], traits)


def own_kernel(power_ref, *refs):
    *banks, out_ref = refs
    scores = [[log_bessel(power_ref[i, q]) for q in range(2)] for i in range(power_ref.shape[0])]
    store_marginal(out_ref, scores, traits_of(banks, power_ref.shape[0] // len(banks)))


def final_kernel(*refs):
    *sides, log_ref, chirp_ref, delay_ref = refs
    rows = (sides[0].shape[0] - 8) // 6
    keep = log_ref.shape[0] // 4
    prior = functools.reduce(jnp.add, [side[6 * rows : 6 * rows + 1, :] for side in sides])
    log_prior = jnp.log(prior)
    for q in range(2):
        logs, chirps, delays = (
            [side[(3 * q + i) * rows : (3 * q + i + 1) * rows, :] for side in sides] for i in range(3)
        )
        peak = functools.reduce(jnp.maximum, logs)
        masses = [jnp.exp(value - peak) for value in logs]
        total = functools.reduce(jnp.add, masses)
        inv = 1.0 / total
        chirp = functools.reduce(jnp.add, [m * value for m, value in zip(masses, chirps)]) * inv
        delay = functools.reduce(jnp.add, [m * value for m, value in zip(masses, delays)]) * inv
        level = peak + jnp.log(total) - log_prior
        for ref, value in ((log_ref, level), (chirp_ref, chirp), (delay_ref, delay)):
            for h in range(2):
                ref[pl.ds(2 * q + h, keep, stride=4), :] = value[:keep, h * LANES : (h + 1) * LANES]


HBM = pl.BlockSpec(memory_space=pltpu.HBM)
VMEM = pl.BlockSpec(memory_space=pltpu.VMEM)


def in_hbm(value):
    return pltpu.with_memory_space_constraint(value, pltpu.HBM)


def params(mib):
    return pltpu.CompilerParams(vmem_limit_bytes=mib * 1024 * 1024)


def halo_routes(segs, n):
    cut = segs // 2 - 1
    if n % 2 or cut < 2:
        return [(i, i + 1) for i in range(segs - 1)], []
    closing = {cut - 1: 0, segs - 1: cut}
    ring = [(i, closing.get(i, i + 1)) for i in range(segs)]
    bridge = []
    for i in range(segs):
        for j in range(n):
            to = (2 * cut - 1 - i) * n + j if i in (cut - 1, cut) else i * n + (j ^ 1)
            bridge.append((i * n + j, to))
    return ring, bridge


def steps(strain, inv_asd, templates, tmpl_len, weights, chirp_mass, valid):
    n = lax.axis_size("bank")
    segs = lax.axis_size("seg")
    count = templates.shape[1]
    rows = strain.shape[0] // LANES
    tail_rows = OVER // LANES
    flags = valid.shape[0]
    group = 2 if n % 2 == 0 else 1
    table = {key: jnp.asarray(value) for key, value in tables(rows // 2, n).items()}
    strain = strain.reshape(rows, LANES)
    asd = inv_asd.reshape(-1, LANES)
    tail, traits, gates = pl.pallas_call(
        tail_kernel,
        in_specs=[HBM] * 5,
        out_specs=[VMEM] * 3,
        out_shape=[
            pltpu.VMEM((tail_rows, LANES), F32),
            pltpu.VMEM((trait_rows(count), FA), F32),
            pltpu.VMEM((flags, LANES), F32),
        ],
        scratch_shapes=[
            pltpu.SMEM((count,), jnp.int32),
            pltpu.SMEM((count,), F32),
            pltpu.SMEM((count,), F32),
            pltpu.SMEM((flags,), jnp.int32),
            pltpu.VMEM((tail_rows, LANES), F32),
            pltpu.SemaphoreType.DMA((5,)),
        ],
        compiler_params=params(4),
        cost_estimate=pl.CostEstimate(flops=4 * 10**9, bytes_accessed=10**5, transcendentals=0),
        name="tail",
    )(*map(in_hbm, (tmpl_len, weights, chirp_mass, valid, strain)))
    ring, bridge = halo_routes(segs, n)
    halos = [lax.ppermute(tail, "seg", ring)]
    if bridge:
        halos.append(lax.ppermute(tail, ("seg", "bank"), bridge))
    bank = pl.pallas_call(
        bank_kernel,
        in_specs=[VMEM] * 3,
        out_specs=VMEM,
        out_shape=pltpu.VMEM((2 * count * FA + trait_rows(count), FA), F32),
        compiler_params=params(8),
        cost_estimate=pl.CostEstimate(flops=10**6, bytes_accessed=10**4, transcendentals=0),
        name="bank",
    )(traits, asd, templates.astype(F32).reshape(2, count, -1, LANES))
    banks = [bank] + [
        lax.ppermute(bank, "bank", [(i, i // group * group + (i + r) % group) for i in range(n)])
        for r in range(1, group)
    ]
    section = pl.pallas_call(
        section_kernel,
        in_specs=[VMEM] * 3,
        out_specs=VMEM,
        out_shape=pltpu.VMEM((2 * FA, FA), F32),
        scratch_shapes=[pltpu.VMEM((rows, LANES), F32)],
        compiler_params=params(12),
        cost_estimate=pl.CostEstimate(flops=10**6, bytes_accessed=10**4, transcendentals=0),
        name="section",
    )(gates, strain, table["first"])
    spec = pl.pallas_call(
        functools.partial(spectrum_kernel, segs=segs),
        in_specs=[VMEM] * (4 + len(halos)),
        out_specs=VMEM,
        out_shape=pltpu.VMEM((2, FA, FA), F32),
        compiler_params=params(10),
        cost_estimate=pl.CostEstimate(flops=10**6, bytes_accessed=10**4, transcendentals=0),
        name="spectrum",
    )(section, table["head"], table["second"], table["twist"], *halos)
    own_rows = padded(rows // 4 // n)
    side = pltpu.VMEM((6 * own_rows + 8, FA), F32)
    powers, *outs = pl.pallas_call(
        functools.partial(main_kernel, group=group),
        in_specs=[VMEM] * (4 + group),
        out_specs=[VMEM] * (n // group),
        out_shape=[pltpu.VMEM((count * group, 2, own_rows, FA), F32)] + [side] * (n // group - 1),
        compiler_params=params(20),
        cost_estimate=pl.CostEstimate(flops=4 * 10**9, bytes_accessed=4 * 10**6, transcendentals=0),
        name="main",
    )(spec, *banks, *(table[key] for key in ("third", "fourth", "twist")))
    sides = [
        lax.ppermute(out, "bank", [(i, partner(i, r, n, group)) for i in range(n)])
        for r, out in enumerate(outs, 1)
    ]
    own = pl.pallas_call(
        own_kernel,
        in_specs=[VMEM] * (1 + group),
        out_specs=VMEM,
        out_shape=side,
        compiler_params=params(6),
        cost_estimate=pl.CostEstimate(flops=10**9, bytes_accessed=10**6, transcendentals=0),
        name="own",
    )(powers, *banks)
    results = pl.pallas_call(
        final_kernel,
        in_specs=[VMEM] * (n // group),
        out_specs=[VMEM] * 3,
        out_shape=[jax.ShapeDtypeStruct((rows // n, LANES), F32)] * 3,
        compiler_params=params(6),
        name="final",
    )(own, *sides)
    return tuple(result.reshape(-1) for result in results)


def solution(mesh):
    placed = (P("seg"), P(), P(None, "bank", None), P("bank"), P("bank"), P("bank"), P("seg"))
    return jax.shard_map(
        steps,
        mesh=mesh,
        in_specs=placed,
        out_specs=(P(("seg", "bank")), P(("seg", "bank")), P(("seg", "bank"))),
        check_vma=False,
    )
```
